32 devices in a mesh: blk: 16 (over z, y, core), grp: 2 (over x).
Axes of the slice: x: 2, y: 2, z: 4, core: 2. Of those that a mesh axis runs over, the one named last changes fastest.
Arguments:
- images: float32 [4096, 768], P(('blk', 'grp')), may hold values from -0.24 to 0.24
- texts: float32 [4096, 768], P(('blk', 'grp')), may hold values from -0.24 to 0.24
- log_temp: float32 [1], replicated, may hold values from 2.3 to 3
- bias: float32 [1], replicated, may hold values from -3 to -1
- row_weight: float32 [4096], P(('blk', 'grp')), may hold values from 0.5 to 2
Outputs:
- row_loss: float32 [4096], P(('blk', 'grp'))
- grad_images: float32 [4096, 768], P(('blk', 'grp'))
- grad_texts: float32 [4096, 768], P(('blk', 'grp'))
The draws below stay inside these ranges and needn't reach their ends.
All inputs are finite; a program needn't handle non-finite values.
Results may differ from the reference program's by a relative error of at most 0.00013.
Values sent between devices are 32-bit elements; how exact they have to be, the bound alone decides.
No kernel may reach another device: no remote copies, remote signals or barrier semaphores. Data moves between devices by JAX's collectives and lax.ppermute only.
A program may use at most 64 MiB of HBM per device.

```python
import math
import jax
import jax.numpy as jnp
from jax import lax

D = 768
ROWS = 128
REACH = 1
PAIRS = 4096
N_BLK = 16
N_GRP = 2


def steps_of(own_key, dims, pieces, least, high):
    def one(dim, blocks):
        draws = jax.random.uniform(jax.random.fold_in(jax.random.fold_in(own_key, 6), dim), (blocks,), jnp.float32, least / len(pieces), high / len(pieces))
        return jnp.repeat(jnp.exp(draws), dims[dim] // blocks).reshape((-1,) + (1,) * (len(dims) - dim - 1))

    loudness = one(*pieces[0])
    for cut in pieces[1:]:
        loudness = loudness * one(*cut)
    return loudness


def gaussian(rng, shape, width, most, cuts=(), kind=jnp.bfloat16):
    result = jax.random.normal(rng, shape, jnp.float32) * width
    if len(cuts) > 0:
        result = steps_of(rng, shape, cuts, -0.22, 0.18) * result
    return jnp.clip(result, min=-most, max=most).astype(kind)


def setup_inputs(seed: int = 0) -> dict:
    streams_of = jax.random.split(jax.random.key(seed), 6)
    return {
        "images": gaussian(streams_of[0], (PAIRS, D), 0.04, 0.24, ((0, 32),), jnp.float32),
        "texts": gaussian(streams_of[1], (PAIRS, D), 0.04, 0.24, ((0, 32),), jnp.float32),
        "log_temp": jnp.clip(jax.random.uniform(streams_of[2], (1,), jnp.float32, 2.3, 3.0), 2.3, 3.0),
        "bias": jnp.clip(jax.random.uniform(streams_of[3], (1,), jnp.float32, -3.0, -1.0), -3.0, -1.0),
        "row_weight": jnp.clip(jnp.exp(math.log(2.0) - 1.3862944 * jax.random.uniform(streams_of[4], (PAIRS,), jnp.float32) ** steps_of(streams_of[4], (PAIRS,), ((0, 32),), -0.2, 0.2)), 0.5, 2.0),
    }


def normed(values):
    return values * lax.rsqrt(lax.optimization_barrier(jnp.sum(values * values, axis=1, keepdims=True)) + 1e-06)

def reference(images, texts, log_temp, bias, row_weight):
    group = ROWS * N_GRP

    def forward(images, texts):
        unit_x = normed(images).reshape(N_BLK, group, D)
        unit_y = normed(texts).reshape(N_BLK, group, D)
        temper = jnp.exp(log_temp[0])
        same = jnp.eye(group, dtype=bool)
        total = jnp.zeros((N_BLK, group), jnp.float32)
        for offset in range(-REACH, REACH + 1):
            other = jnp.roll(unit_y, -offset, axis=0)
            logits = temper * jnp.einsum('bid,bjd->bij', unit_x, other, precision=lax.Precision.HIGHEST) + bias[0]
            if offset == 0:
                labels = jnp.where(same, 1.0, -1.0)
            else:
                labels = -1.0
            total = total + lax.optimization_barrier(jnp.sum(jax.nn.softplus(-labels * logits), axis=2))
        sums = total.reshape(-1)
        return (jnp.sum(row_weight * sums), sums)
    (value, sums), grads = jax.value_and_grad(forward, argnums=(0, 1), has_aux=True)(images, texts)
    row_loss = sums / ((2 * REACH + 1) * group)
    return (row_loss, grads[0], grads[1])
```

```python
import jax
import jax.numpy as jnp
from jax import lax
from jax.sharding import PartitionSpec as P

HIGH = lax.Precision.HIGH


def swapped(x, axis, near):
    length = lax.axis_size(axis)
    if near:
        pairs = [(i, i + 1) for i in range(0, length, 2)]
    else:
        pairs = [(i, (i + 1) % length) for i in range(1, length, 2)]
    return lax.ppermute(x, axis, pairs + [(b, a) for (a, b) in pairs])


def shifted(x, axis, by):
    length = lax.axis_size(axis)
    return lax.ppermute(x, axis, [(i, (i + by) % length) for i in range(length)])


def normed(values):
    scale = lax.rsqrt(jnp.sum(values * values, axis=1, keepdims=True) + 1e-06)
    return (values * scale, scale)


def unnormed(grad, unit, scale):
    return scale * (grad - unit * jnp.sum(unit * grad, axis=1, keepdims=True))


def tile_terms(left, right, temper, offset_b, weight, positive):
    logits = temper * jnp.einsum("id,jd->ij", left, right, precision=HIGH) + offset_b
    signed = logits if positive is None else jnp.where(positive, -logits, logits)
    losses = jax.nn.softplus(signed)
    slope = jax.nn.sigmoid(signed) * weight[:, None]
    if positive is not None:
        slope = jnp.where(positive, -slope, slope)
    return (jnp.sum(losses, axis=1), slope)


def shards(images, texts, log_temp, bias, row_weight):
    members = lax.axis_size("grp")
    count = images.shape[0]
    rows_i = [images] + [shifted(images, "grp", -s) for s in range(1, members)]
    weights = [row_weight] + [shifted(row_weight, "grp", -s) for s in range(1, members)]
    far = swapped(texts, "blk", False)
    near = swapped(texts, "blk", True)
    temper = jnp.exp(log_temp[0])
    offset_b = bias[0]
    unit_y, scale_y = normed(texts)
    unit_near, _ = normed(near)
    unit_far, _ = normed(far)
    units_x, scales_x = zip(*[normed(r) for r in rows_i])
    eye = lax.broadcasted_iota(jnp.int32, (count, count), 0) == lax.broadcasted_iota(
        jnp.int32, (count, count), 1
    )
    texts_all = [unit_y, unit_near, unit_far]
    grad_t = [None, None, None]
    grads_x = []
    sums_x = []
    for s in range(members):
        total = None
        grad = None
        for t in range(3):
            positive = eye if (s == 0 and t == 0) else None
            part, slope = tile_terms(
                units_x[s], texts_all[t], temper, offset_b, weights[s], positive
            )
            slope = slope * temper
            total = part if total is None else total + part
            g = jnp.dot(slope, texts_all[t], precision=HIGH)
            grad = g if grad is None else grad + g
            h = jnp.einsum("ij,id->jd", slope, units_x[s], precision=HIGH)
            grad_t[t] = h if grad_t[t] is None else grad_t[t] + h
        grads_x.append(grad)
        sums_x.append(total)
    back_far = swapped(grad_t[2], "blk", False)
    back_near = swapped(grad_t[1], "blk", True)
    grad_x = grads_x[0]
    sums = sums_x[0]
    for s in range(1, members):
        grad_x = grad_x + shifted(grads_x[s], "grp", s)
        sums = sums + shifted(sums_x[s], "grp", s)
    grad_y = grad_t[0] + back_near + back_far
    row_loss = sums / (3 * members * count)
    return (row_loss, unnormed(grad_x, units_x[0], scales_x[0]), unnormed(grad_y, unit_y, scale_y))


def solution(mesh):
    placed = (P(("blk", "grp"), None), P(("blk", "grp"), None), P(), P(), P(("blk", "grp")))
    return jax.shard_map(
        shards,
        mesh=mesh,
        in_specs=placed,
        out_specs=(P(("blk", "grp")), P(("blk", "grp"), None), P(("blk", "grp"), None)),
        check_vma=False,
    )
```

```python
import functools

import jax
import jax.numpy as jnp
from jax import lax
from jax.experimental import pallas as pl
from jax.experimental.pallas import tpu as pltpu
from jax.sharding import PartitionSpec as P

BF = jnp.bfloat16
F32 = jnp.float32
VMEM = pl.BlockSpec(memory_space=pltpu.VMEM)
SMEM = pl.BlockSpec(memory_space=pltpu.SMEM)


def swapped(x, axis, near):
    length = lax.axis_size(axis)
    if near:
        pairs = [(i, i + 1) for i in range(0, length, 2)]
    else:
        pairs = [(i, (i + 1) % length) for i in range(1, length, 2)]
    return lax.ppermute(x, axis, pairs + [(b, a) for (a, b) in pairs])


def shifted(x, axis, by):
    length = lax.axis_size(axis)
    return lax.ppermute(x, axis, [(i, (i + by) % length) for i in range(length)])


def unit_of(raw):
    return raw * lax.rsqrt(jnp.sum(raw * raw, axis=1, keepdims=True) + 1e-06)


def split(v):
    high = v.astype(BF)
    return high, (v - high.astype(F32)).astype(BF)


def dot3(a, b, dims):
    def one(p, q):
        return lax.dot_general(p, q, (dims, ((), ())), preferred_element_type=F32)

    return one(a[0], b[0]) + (one(a[0], b[1]) + one(a[1], b[0]))


def scores(texts, images, temper, bias):
    return temper * dot3(texts, images, ((1,), (1,))) + bias


def terms(signed):
    small = jnp.exp(-jnp.abs(signed))
    loss = jnp.maximum(signed, 0.0) + jnp.log1p(small)
    gate = jnp.where(signed >= 0.0, 1.0, small) / (1.0 + small)
    return loss, gate


def slopes(texts, images, temper, bias, weight, diagonal=None):
    signed = scores(texts, images, temper, bias)
    if diagonal is not None:
        signed = jnp.where(diagonal, -signed, signed)
    loss, gate = terms(signed)
    slope = gate * weight
    if diagonal is not None:
        slope = jnp.where(diagonal, -slope, slope)
    return jnp.sum(loss, axis=0, keepdims=True), split(slope)


def joined(*pairs):
    return tuple(jnp.concatenate(p, axis=0) for p in zip(*pairs))


def part(pair, low, high):
    return pair[0][low:high], pair[1][low:high]


ON_ROWS = ((1,), (0,))
ON_COLS = ((0,), (0,))


def first_body(lt, bi, x_ref, y_ref, near_ref, w_ref, xs_ref, ys_ref, gx_ref, gy_ref, sum_ref):
    temper = jnp.exp(jnp.full((1, 1), lt[0], F32))
    bias = bi[0]
    count = x_ref.shape[0]
    weight = w_ref[...] * temper
    xs = split(unit_of(x_ref[...]))
    xs_ref[0], xs_ref[1] = xs
    own = split(unit_of(y_ref[...]))
    near = split(unit_of(near_ref[...]))
    ys = joined(own, near)
    ys_ref[0], ys_ref[1] = ys
    rows = lax.broadcasted_iota(jnp.int32, (2 * count, count), 0)
    cols = lax.broadcasted_iota(jnp.int32, (2 * count, count), 1)
    sums, slope = slopes(ys, xs, temper, bias, weight, rows == cols)
    sum_ref[...] = sums
    gx_ref[...] = dot3(slope, ys, ON_COLS)
    gy_ref[...] = dot3(slope, xs, ON_ROWS)


def second_body(others, lt, bi, *refs):
    raw_refs, refs = refs[:others], refs[others:]
    w_refs, refs = refs[: others + 1], refs[others + 1 :]
    far_ref, xs_ref, ys_ref, sum_in, refs = *refs[:4], refs[4:]
    gfar_ref, refs = refs[0], refs[1:]
    gp_refs, refs = refs[:others], refs[others:]
    sump_refs, refs = refs[:others], refs[others:]
    sum_ref, px_ref, ps_ref, fars_ref, fs_ref = refs
    temper = jnp.exp(jnp.full((1, 1), lt[0], F32))
    bias = bi[0]
    count = far_ref.shape[0]
    xs = (xs_ref[0], xs_ref[1])
    far = split(unit_of(far_ref[...]))
    fars_ref[0], fars_ref[1] = far
    ys = joined((ys_ref[0], ys_ref[1]), far)
    sums, slope = slopes(far, xs, temper, bias, w_refs[0][...] * temper)
    sum_ref[...] = sum_in[...] + sums
    fs_ref[0], fs_ref[1] = slope
    g_far = dot3(slope, xs, ON_ROWS)
    for s in range(others):
        xp = split(unit_of(raw_refs[s][...]))
        px_ref[s, 0], px_ref[s, 1] = xp
        sums, slope = slopes(ys, xp, temper, bias, w_refs[s + 1][...] * temper)
        sump_refs[s][...] = sums
        gp_refs[s][...] = dot3(slope, ys, ON_COLS)
        g_far = g_far + dot3(part(slope, 2 * count, 3 * count), xp, ON_ROWS)
        ps_ref[s, 0], ps_ref[s, 1] = part(slope, 0, 2 * count)
    gfar_ref[...] = g_far


def third_body(others, gx_in, gy_in, px_ref, ps_ref, fars_ref, fs_ref, gx_ref, gown_ref, gnear_ref):
    count = gx_in.shape[0]
    gy = gy_in[...]
    for s in range(others):
        gy = gy + dot3((ps_ref[s, 0], ps_ref[s, 1]), (px_ref[s, 0], px_ref[s, 1]), ON_ROWS)
    gown_ref[...] = gy[:count]
    gnear_ref[...] = gy[count:]
    gx_ref[...] = gx_in[...] + dot3((fs_ref[0], fs_ref[1]), (fars_ref[0], fars_ref[1]), ON_COLS)


def last_body(raw_ref, *refs):
    raw = raw_ref[...]
    grad = refs[0][...]
    for r in refs[1:-1]:
        grad = grad + r[...]
    scale = lax.rsqrt(jnp.sum(raw * raw, axis=1, keepdims=True) + 1e-06)
    unit = raw * scale
    refs[-1][...] = scale * (grad - unit * jnp.sum(unit * grad, axis=1, keepdims=True))


def shape(*dims, kind=F32):
    return jax.ShapeDtypeStruct(dims, kind)


def call(body, outs, count_in, scalars=0, final=False):
    run = pl.pallas_call(
        body,
        out_shape=outs if final else [pltpu.VMEM(o.shape, o.dtype) for o in outs],
        in_specs=[SMEM] * scalars + [VMEM] * count_in,
        out_specs=jax.tree.map(lambda _: VMEM, outs),
        compiler_params=pltpu.CompilerParams(vmem_limit_bytes=16 * 1024 * 1024),
    )

    def go(*args):
        held = [pltpu.with_memory_space_constraint(a, pltpu.VMEM) for a in args[scalars:]]
        return run(*args[:scalars], *held)

    return go


def shards(images, texts, log_temp, bias, row_weight):
    members = lax.axis_size("grp")
    others = members - 1
    count, width = images.shape
    weight = row_weight.reshape(1, count)
    far = swapped(texts, "blk", False)
    near = swapped(texts, "blk", True)
    raws = [shifted(images, "grp", -s) for s in range(1, members)]
    weights = [weight] + [shifted(weight, "grp", -s) for s in range(1, members)]
    full = shape(count, width)
    line = shape(1, count)
    xs, ys, gx, gy, sums = call(
        first_body,
        [
            shape(2, count, width, kind=BF),
            shape(2, 2 * count, width, kind=BF),
            full,
            shape(2 * count, width),
            line,
        ],
        4,
        2,
    )(log_temp, bias, images, texts, near, weight)
    outs = call(
        functools.partial(second_body, others),
        [full]
        + [full] * others
        + [line] * others
        + [
            line,
            shape(others, 2, count, width, kind=BF),
            shape(others, 2, 2 * count, count, kind=BF),
            shape(2, count, width, kind=BF),
            shape(2, count, count, kind=BF),
        ],
        2 * others + 5,
        2,
    )(log_temp, bias, *raws, *weights, far, xs, ys, sums)
    g_far, outs = outs[0], outs[1:]
    g_others, outs = outs[:others], outs[others:]
    s_others, outs = outs[:others], outs[others:]
    sums, px, ps, fars, fs = outs
    back_x = [shifted(g_others[s - 1], "grp", s) for s in range(1, members)]
    back_far = swapped(g_far, "blk", False)
    gx, g_own, g_near = call(functools.partial(third_body, others), [full, full, full], 6)(
        gx, gy, px, ps, fars, fs
    )
    back_near = swapped(g_near, "blk", True)
    for s in range(1, members):
        sums = sums + shifted(s_others[s - 1], "grp", s)
    row_loss = (sums / (3 * members * count)).reshape(count)
    grad_x = call(last_body, full, 2 + others, final=True)(images, gx, *back_x)
    grad_y = call(last_body, full, 4, final=True)(texts, g_own, back_near, back_far)
    return (row_loss, grad_x, grad_y)


def solution(mesh):
    placed = (P(("blk", "grp"), None), P(("blk", "grp"), None), P(), P(), P(("blk", "grp")))
    return jax.shard_map(
        shards,
        mesh=mesh,
        in_specs=placed,
        out_specs=(P(("blk", "grp")), P(("blk", "grp"), None), P(("blk", "grp"), None)),
        check_vma=False,
    )
```

```python
import functools

import jax
import jax.numpy as jnp
from jax import lax
from jax.experimental import pallas as pl
from jax.experimental.pallas import tpu as pltpu
from jax.sharding import PartitionSpec as P


BF = jnp.bfloat16
F32 = jnp.float32
VMEM = pl.BlockSpec(memory_space=pltpu.VMEM)
SMEM = pl.BlockSpec(memory_space=pltpu.SMEM)
ANY = pl.BlockSpec(memory_space=pl.ANY)
CHUNKS = 4
NT = ((1,), (1,))
NN = ((1,), (0,))


def swapped(x, axis, near):
    length = lax.axis_size(axis)
    if near:
        pairs = [(i, i + 1) for i in range(0, length, 2)]
    else:
        pairs = [(i, (i + 1) % length) for i in range(1, length, 2)]
    return lax.ppermute(x, axis, pairs + [(b, a) for (a, b) in pairs])


def shifted(x, axis, by):
    length = lax.axis_size(axis)
    return lax.ppermute(x, axis, [(i, (i + by) % length) for i in range(length)])


def unit_of(raw):
    return raw * lax.rsqrt(jnp.sum(raw * raw, axis=1, keepdims=True) + 1e-06)


def stacked(v):
    high = v.astype(BF)
    return jnp.concatenate([high, (v - high.astype(F32)).astype(BF)], axis=0)


def mm(a, b, dims):
    rows = a.shape[0] // 2
    deep = b.shape[0] // 2

    def one(p, q):
        return lax.dot_general(p, q, (dims, ((), ())), preferred_element_type=F32)

    both = one(a[...], b[:deep])
    return both[:rows] + (both[rows:] + one(a[:rows], b[deep:]))


def gated(z, weight, diagonal=None):
    signed = z if diagonal is None else jnp.where(diagonal, -z, z)
    small = jnp.exp(-jnp.abs(signed))
    loss = jnp.maximum(signed, 0.0) + jnp.log1p(small)
    slope = jnp.where(signed >= 0.0, 1.0, small) / (1.0 + small) * weight
    if diagonal is not None:
        slope = jnp.where(diagonal, -slope, slope)
    return jnp.sum(loss, axis=0, keepdims=True), slope


def temper_of(lt):
    return jnp.exp(jnp.full((1, 1), lt[0], F32))


def first_body(lt, bi, x_ref, y_ref, near_ref, w_ref, xs_ref, ys_ref, gx_ref, gy_ref, sum_ref):
    temper = temper_of(lt)
    count = x_ref.shape[0]
    xs_ref[...] = stacked(unit_of(x_ref[...]))
    ys = jnp.concatenate([unit_of(y_ref[...]), unit_of(near_ref[...])], axis=0)
    ys_ref[...] = stacked(ys)
    rows = lax.broadcasted_iota(jnp.int32, (2 * count, count), 0)
    cols = lax.broadcasted_iota(jnp.int32, (2 * count, count), 1)
    z = temper * mm(ys_ref, xs_ref, NT) + bi[0]
    sums, slope = gated(z, w_ref[...] * temper, rows == cols)
    sum_ref[...] = sums
    gx_ref[...] = mm(stacked(slope.T), ys_ref, NN)
    gy_ref[...] = mm(stacked(slope), xs_ref, NN)


def second_body(others, lt, bi, *refs):
    raw_refs, refs = refs[:others], refs[others:]
    w_refs, refs = refs[:others], refs[others:]
    ys_ref, gy_in, refs = refs[0], refs[1], refs[2:]
    px_refs, refs = refs[:others], refs[others:]
    gp_refs, refs = refs[:others], refs[others:]
    sump_refs, refs = refs[:others], refs[others:]
    gown_ref, gnear_ref = refs
    temper = temper_of(lt)
    count = raw_refs[0].shape[0]
    gy = gy_in[...]
    for s in range(others):
        px_refs[s][...] = stacked(unit_of(raw_refs[s][...]))
        z = temper * mm(ys_ref, px_refs[s], NT) + bi[0]
        sump_refs[s][...], slope = gated(z, w_refs[s][...] * temper)
        gp_refs[s][...] = mm(stacked(slope.T), ys_ref, NN)
        gy = gy + mm(stacked(slope), px_refs[s], NN)
    gown_ref[...] = gy[:count]
    gnear_ref[...] = gy[count:]


def third_body(others, lt, bi, *refs):
    members = others + 1
    far_ref, refs = refs[0], refs[1:]
    w_refs, refs = refs[:members], refs[members:]
    x_refs, refs = refs[:members], refs[members:]
    gp_in, refs = refs[:others], refs[others:]
    sum_in, refs = refs[:members], refs[members:]
    gfar_ref, refs = refs[0], refs[1:]
    gp_refs, refs = refs[:others], refs[others:]
    sum_refs, refs = refs[:members], refs[members:]
    fs_ref, slope_ref = refs
    temper = temper_of(lt)
    fs_ref[...] = stacked(unit_of(far_ref[...]))
    gfar = None
    for s in range(members):
        z = temper * mm(fs_ref, x_refs[s], NT) + bi[0]
        sums, slope = gated(z, w_refs[s][...] * temper)
        sum_refs[s][...] = sum_in[s][...] + sums
        g = mm(stacked(slope), x_refs[s], NN)
        gfar = g if gfar is None else gfar + g
        if s == 0:
            slope_ref[...] = stacked(slope.T)
        else:
            gp_refs[s - 1][...] = gp_in[s - 1][...] + mm(stacked(slope.T), fs_ref, NN)
    gfar_ref[...] = gfar


def fourth_body(gx_in, slope_ref, fs_ref, gx_ref):
    gx_ref[...] = gx_in[...] + mm(slope_ref, fs_ref, NN)


def last_body(terms, sums, pairs, raw_ref, *refs):
    grads, refs = refs[:terms], refs[terms:]
    lines, refs = refs[:sums], refs[sums:]
    out_ref, refs = refs[0], refs[1:]
    if sums:
        total = lines[0][...]
        for r in lines[1:]:
            total = total + r[...]
        refs[0][...] = total / pairs
        refs = refs[1:]
    held, sem = refs
    rows = raw_ref.shape[0] // CHUNKS
    copies = []
    for c in range(CHUNKS):
        here = pl.ds(c * rows, rows)
        raw = raw_ref[here, :]
        grad = grads[0][here, :]
        for r in grads[1:]:
            grad = grad + r[here, :]
        scale = lax.rsqrt(jnp.sum(raw * raw, axis=1, keepdims=True) + 1e-06)
        unit = raw * scale
        held[here, :] = scale * (grad - unit * jnp.sum(unit * grad, axis=1, keepdims=True))
        copies.append(pltpu.make_async_copy(held.at[here, :], out_ref.at[here, :], sem.at[c]))
        copies[-1].start()
    for copy in copies:
        copy.wait()


def shape(*dims, kind=F32):
    return jax.ShapeDtypeStruct(dims, kind)


PARAMS = pltpu.CompilerParams(vmem_limit_bytes=16 * 1024 * 1024)


def in_vmem(args):
    return [pltpu.with_memory_space_constraint(a, pltpu.VMEM) for a in args]


def call(body, outs, scalars, *args):
    return pl.pallas_call(
        body,
        out_shape=[pltpu.VMEM(o.shape, o.dtype) for o in outs],
        in_specs=[SMEM] * len(scalars) + [VMEM] * len(args),
        out_specs=[VMEM] * len(outs),
        compiler_params=PARAMS,
    )(*scalars, *in_vmem(args))


def finish(raw, grads, lines, pairs):
    like = jax.ShapeDtypeStruct(raw.shape, raw.dtype)
    line = shape(1, raw.shape[0])
    return pl.pallas_call(
        functools.partial(last_body, len(grads), len(lines), pairs),
        out_shape=[like, line] if lines else [like],
        in_specs=[VMEM] * (1 + len(grads) + len(lines)),
        out_specs=[ANY, VMEM] if lines else [ANY],
        scratch_shapes=[pltpu.VMEM(raw.shape, F32), pltpu.SemaphoreType.DMA((CHUNKS,))],
        compiler_params=PARAMS,
    )(*in_vmem([raw, *grads, *lines]))


def body(images, texts, log_temp, bias, row_weight):
    members = lax.axis_size("grp")
    others = members - 1
    count, width = images.shape
    weight = row_weight.reshape(1, count)
    scalars = (log_temp, bias)
    raws = [shifted(images, "grp", -s) for s in range(1, members)]
    far = swapped(texts, "blk", False)
    near = swapped(texts, "blk", True)
    weights = [weight] + [shifted(weight, "grp", -s) for s in range(1, members)]
    full = shape(count, width)
    line = shape(1, count)
    stack = shape(2 * count, width, kind=BF)
    xs, ys, gx, gy, sums = call(
        first_body,
        [stack, shape(4 * count, width, kind=BF), full, shape(2 * count, width), line],
        scalars,
        images,
        texts,
        near,
        weight,
    )
    outs = call(
        functools.partial(second_body, others),
        [stack] * others + [full] * others + [line] * others + [full, full],
        scalars,
        *raws,
        *weights[1:],
        ys,
        gy,
    )
    px, outs = outs[:others], outs[others:]
    gp, outs = outs[:others], outs[others:]
    sump, (g_own, g_near) = outs[:others], outs[others:]
    back_near = swapped(g_near, "blk", True)
    outs = call(
        functools.partial(third_body, others),
        [full]
        + [full] * others
        + [line] * members
        + [stack, shape(2 * count, count, kind=BF)],
        scalars,
        far,
        *weights,
        xs,
        *px,
        *gp,
        sums,
        *sump,
    )
    g_far, outs = outs[0], outs[1:]
    gp, outs = outs[:others], outs[others:]
    sums, (fs, slope) = outs[:members], outs[members:]
    back_far = swapped(g_far, "blk", False)
    back_x = [shifted(gp[s - 1], "grp", s) for s in range(1, members)]
    back_sum = [shifted(sums[s], "grp", s) for s in range(1, members)]
    gx = call(fourth_body, [full], (), gx, slope, fs)[0]
    grad_x, row_loss = finish(images, [gx, *back_x], [sums[0], *back_sum], 3.0 * members * count)
    grad_y = finish(texts, [g_own, back_near, back_far], [], None)[0]
    return (row_loss.reshape(count), grad_x, grad_y)


def solution(mesh):
    placed = (P(("blk", "grp"), None), P(("blk", "grp"), None), P(), P(), P(("blk", "grp")))
    return jax.shard_map(
        body,
        mesh=mesh,
        in_specs=placed,
        out_specs=(P(("blk", "grp")), P(("blk", "grp"), None), P(("blk", "grp"), None)),
        check_vma=False,
    )
```

```python
import functools

import jax
import jax.numpy as jnp
from jax import lax
from jax.experimental import pallas as pl
from jax.experimental.pallas import tpu as pltpu
from jax.sharding import PartitionSpec as P


BF = jnp.bfloat16
F32 = jnp.float32
VMEM = pl.BlockSpec(memory_space=pltpu.VMEM)
SMEM = pl.BlockSpec(memory_space=pltpu.SMEM)
HBM = pl.BlockSpec(memory_space=pltpu.HBM)
CHUNKS = 4
NT = ((1,), (1,))
NN = ((1,), (0,))


def swapped(x, axis, near):
    length = lax.axis_size(axis)
    if near:
        pairs = [(i, i + 1) for i in range(0, length, 2)]
    else:
        pairs = [(i, (i + 1) % length) for i in range(1, length, 2)]
    return lax.ppermute(x, axis, pairs + [(b, a) for (a, b) in pairs])


def shifted(x, axis, by):
    length = lax.axis_size(axis)
    return lax.ppermute(x, axis, [(i, (i + by) % length) for i in range(length)])


def unit_of(raw):
    return raw * lax.rsqrt(jnp.sum(raw * raw, axis=1, keepdims=True) + 1e-06)


def stacked(v):
    high = v.astype(BF)
    return jnp.concatenate([high, (v - high.astype(F32)).astype(BF)], axis=0)


def mm(a, b, dims):
    rows = a.shape[0] // 2
    deep = b.shape[0] // 2

    def one(p, q):
        return lax.dot_general(p, q, (dims, ((), ())), preferred_element_type=F32)

    both = one(a[...], b[:deep])
    return both[:rows] + (both[rows:] + one(a[:rows], b[deep:]))


def log_one_plus(t):
    series = t * (1.0 + t * (-0.5 + t * (1.0 / 3.0 + t * (-0.25 + t * 0.2))))
    return jnp.where(t < 0.03125, series, jnp.log(1.0 + t))


def gated(z, weight, diagonal=None):
    signed = z if diagonal is None else jnp.where(diagonal, -z, z)
    small = jnp.exp(-jnp.abs(signed))
    loss = jnp.maximum(signed, 0.0) + log_one_plus(small)
    slope = jnp.where(signed >= 0.0, 1.0, small) / (1.0 + small) * weight
    if diagonal is not None:
        slope = jnp.where(diagonal, -slope, slope)
    return jnp.sum(loss, axis=0, keepdims=True), slope


def temper_of(lt):
    return jnp.exp(jnp.full((1, 1), lt[0], F32))


def first_body(lt, bi, x_any, y_any, near_ref, w_ref, *refs):
    x_ref, y_ref, xs_ref, ys_ref, gx_ref, gy_ref, sum_ref, sem = refs
    copies = [
        pltpu.make_async_copy(x_any, x_ref, sem.at[0]),
        pltpu.make_async_copy(y_any, y_ref, sem.at[1]),
    ]
    for copy in copies:
        copy.start()
    temper = temper_of(lt)
    count = near_ref.shape[0]
    near = unit_of(near_ref[...])
    copies[0].wait()
    xs_ref[...] = stacked(unit_of(x_ref[...]))
    copies[1].wait()
    ys_ref[...] = stacked(jnp.concatenate([unit_of(y_ref[...]), near], axis=0))
    rows = lax.broadcasted_iota(jnp.int32, (2 * count, count), 0)
    cols = lax.broadcasted_iota(jnp.int32, (2 * count, count), 1)
    z = temper * mm(ys_ref, xs_ref, NT) + bi[0]
    sums, slope = gated(z, w_ref[...] * temper, rows == cols)
    sum_ref[...] = sums
    gx_ref[...] = mm(stacked(slope.T), ys_ref, NN)
    gy_ref[...] = mm(stacked(slope), xs_ref, NN)


def second_body(others, lt, bi, *refs):
    raw_refs, refs = refs[:others], refs[others:]
    w_refs, refs = refs[:others], refs[others:]
    ys_ref, refs = refs[0], refs[1:]
    px_refs, refs = refs[:others], refs[others:]
    gp_refs, refs = refs[:others], refs[others:]
    sump_refs, slope_refs = refs[:others], refs[others:]
    temper = temper_of(lt)
    for s in range(others):
        px_refs[s][...] = stacked(unit_of(raw_refs[s][...]))
        z = temper * mm(ys_ref, px_refs[s], NT) + bi[0]
        sump_refs[s][...], slope = gated(z, w_refs[s][...] * temper)
        slope_refs[s][...] = slope
        gp_refs[s][...] = mm(stacked(slope.T), ys_ref, NN)


def third_body(others, lt, bi, *refs):
    members = others + 1
    far_ref, refs = refs[0], refs[1:]
    w_refs, refs = refs[:members], refs[members:]
    x_refs, refs = refs[:members], refs[members:]
    gp_in, refs = refs[:others], refs[others:]
    sum_in, refs = refs[:members], refs[members:]
    gfar_ref, refs = refs[0], refs[1:]
    gp_refs, refs = refs[:others], refs[others:]
    sum_refs, refs = refs[:members], refs[members:]
    fs_ref, slope_ref = refs
    temper = temper_of(lt)
    fs_ref[...] = stacked(unit_of(far_ref[...]))
    gfar = None
    for s in range(members):
        z = temper * mm(fs_ref, x_refs[s], NT) + bi[0]
        sums, slope = gated(z, w_refs[s][...] * temper)
        sum_refs[s][...] = sum_in[s][...] + sums
        g = mm(stacked(slope), x_refs[s], NN)
        gfar = g if gfar is None else gfar + g
        if s == 0:
            slope_ref[...] = slope
        else:
            gp_refs[s - 1][...] = gp_in[s - 1][...] + mm(stacked(slope.T), fs_ref, NN)
    gfar_ref[...] = gfar


def fourth_body(others, gx_in, gy_in, slope_ref, fs_ref, *refs):
    slopes, refs = refs[:others], refs[others:]
    px_refs, (gx_ref, gown_ref, gnear_ref) = refs[:others], refs[others:]
    count = gx_in.shape[0]
    gy = gy_in[...]
    for s in range(others):
        gy = gy + mm(stacked(slopes[s][...]), px_refs[s], NN)
    gown_ref[...] = gy[:count]
    gnear_ref[...] = gy[count:]
    gx_ref[...] = gx_in[...] + mm(stacked(slope_ref[...].T), fs_ref, NN)


def last_body(parts, lines, pairs, *refs):
    held, line, sem = refs[-3:]
    refs, outs = refs[:-6], refs[-6:-3]
    copies = []

    def send(source, target):
        copies.append(pltpu.make_async_copy(source, target, sem.at[len(copies)]))
        copies[-1].start()

    for k, terms in enumerate(parts):
        raw_ref, grads, refs = refs[0], refs[1 : 1 + terms], refs[1 + terms :]
        rows = raw_ref.shape[0] // CHUNKS
        for c in range(CHUNKS):
            here = pl.ds(c * rows, rows)
            raw = raw_ref[here, :]
            grad = grads[0][here, :]
            for r in grads[1:]:
                grad = grad + r[here, :]
            scale = lax.rsqrt(jnp.sum(raw * raw, axis=1, keepdims=True) + 1e-06)
            unit = raw * scale
            inner = jnp.sum(unit * grad, axis=1, keepdims=True)
            held[k, here, :] = scale * (grad - unit * inner)
            send(held.at[k, here, :], outs[k].at[here, :])
    total = refs[0][...]
    for r in refs[1:lines]:
        total = total + r[...]
    line[...] = total / pairs
    send(line, outs[2])
    for copy in copies:
        copy.wait()


def shape(*dims, kind=F32):
    return jax.ShapeDtypeStruct(dims, kind)


PARAMS = pltpu.CompilerParams(vmem_limit_bytes=16 * 1024 * 1024)


def in_hbm(args):
    return [pltpu.with_memory_space_constraint(a, pltpu.HBM) for a in args]


def in_vmem(args):
    return [pltpu.with_memory_space_constraint(a, pltpu.VMEM) for a in args]


def call(body, outs, scalars, *args, scratch=(), anywhere=0):
    return pl.pallas_call(
        body,
        out_shape=[pltpu.VMEM(o.shape, o.dtype) for o in outs],
        in_specs=[SMEM] * len(scalars) + [HBM] * anywhere + [VMEM] * (len(args) - anywhere),
        out_specs=[VMEM] * len(outs),
        scratch_shapes=list(scratch),
        compiler_params=PARAMS,
    )(*scalars, *in_hbm(args[:anywhere]), *in_vmem(args[anywhere:]))


def finish(x_terms, y_terms, lines, pairs):
    full = shape(*x_terms[0].shape)
    line = shape(1, full.shape[0])
    args = [*x_terms, *y_terms, *lines]
    return pl.pallas_call(
        functools.partial(last_body, (len(x_terms) - 1, len(y_terms) - 1), len(lines), pairs),
        out_shape=[full, full, line],
        in_specs=[VMEM] * len(args),
        out_specs=[HBM] * 3,
        scratch_shapes=[
            pltpu.VMEM((2, *full.shape), F32),
            pltpu.VMEM(line.shape, F32),
            pltpu.SemaphoreType.DMA((2 * CHUNKS + 1,)),
        ],
        compiler_params=PARAMS,
    )(*in_vmem(args))


def body(images, texts, log_temp, bias, row_weight):
    members = lax.axis_size("grp")
    others = members - 1
    count, width = images.shape
    weight = row_weight.reshape(1, count)
    scalars = (log_temp, bias)
    raws = [shifted(images, "grp", -s) for s in range(1, members)]
    far = swapped(texts, "blk", False)
    near = swapped(texts, "blk", True)
    weights = [weight] + [shifted(weight, "grp", -s) for s in range(1, members)]
    full = shape(count, width)
    line = shape(1, count)
    stack = shape(2 * count, width, kind=BF)
    x_raw, y_raw, xs, ys, gx, gy, sums = call(
        first_body,
        [
            full,
            full,
            stack,
            shape(4 * count, width, kind=BF),
            full,
            shape(2 * count, width),
            line,
        ],
        scalars,
        images,
        texts,
        near,
        weight,
        scratch=[pltpu.SemaphoreType.DMA((2,))],
        anywhere=2,
    )
    outs = call(
        functools.partial(second_body, others),
        [stack] * others
        + [full] * others
        + [line] * others
        + [shape(2 * count, count)] * others,
        scalars,
        *raws,
        *weights[1:],
        ys,
    )
    px, outs = outs[:others], outs[others:]
    gp, outs = outs[:others], outs[others:]
    sump, slopes = outs[:others], outs[others:]
    outs = call(
        functools.partial(third_body, others),
        [full]
        + [full] * others
        + [line] * members
        + [stack, shape(count, count)],
        scalars,
        far,
        *weights,
        xs,
        *px,
        *gp,
        sums,
        *sump,
    )
    g_far, outs = outs[0], outs[1:]
    gp, outs = outs[:others], outs[others:]
    sums, (fs, slope) = outs[:members], outs[members:]
    back_far = swapped(g_far, "blk", False)
    back_x = [shifted(gp[s - 1], "grp", s) for s in range(1, members)]
    back_sum = [shifted(sums[s], "grp", s) for s in range(1, members)]
    gx, g_own, g_near = call(
        functools.partial(fourth_body, others),
        [full] * 3,
        (),
        gx,
        gy,
        slope,
        fs,
        *slopes,
        *px,
    )
    back_near = swapped(g_near, "blk", True)
    grad_x, grad_y, row_loss = finish(
        [x_raw, gx, *back_x],
        [y_raw, g_own, back_near, back_far],
        [sums[0], *back_sum],
        3.0 * members * count,
    )
    return (row_loss.reshape(count), grad_x, grad_y)


def solution(mesh):
    placed = (P(("blk", "grp"), None), P(("blk", "grp"), None), P(), P(), P(("blk", "grp")))
    return jax.shard_map(
        body,
        mesh=mesh,
        in_specs=placed,
        out_specs=(P(("blk", "grp")), P(("blk", "grp"), None), P(("blk", "grp"), None)),
        check_vma=False,
    )
```

```python
import functools

import jax
import jax.numpy as jnp
from jax import lax
from jax.experimental import pallas as pl
from jax.experimental.pallas import tpu as pltpu
from jax.sharding import PartitionSpec as P


BF = jnp.bfloat16
F32 = jnp.float32
VMEM = pl.BlockSpec(memory_space=pltpu.VMEM)
SMEM = pl.BlockSpec(memory_space=pltpu.SMEM)
HBM = pl.BlockSpec(memory_space=pltpu.HBM)
CHUNKS = 4
NT = ((1,), (1,))
NN = ((1,), (0,))


def swapped(x, axis, near):
    length = lax.axis_size(axis)
    if near:
        pairs = [(i, i + 1) for i in range(0, length, 2)]
    else:
        pairs = [(i, (i + 1) % length) for i in range(1, length, 2)]
    return lax.ppermute(x, axis, pairs + [(b, a) for (a, b) in pairs])


def shifted(x, axis, by):
    length = lax.axis_size(axis)
    return lax.ppermute(x, axis, [(i, (i + by) % length) for i in range(length)])


def stacked(v):
    high = v.astype(BF)
    return jnp.concatenate([high, (v - high.astype(F32)).astype(BF)], axis=0)


def mm(a, b, dims):
    rows = a.shape[0] // 2
    deep = b.shape[0] // 2

    def one(p, q):
        return lax.dot_general(p, q, (dims, ((), ())), preferred_element_type=F32)

    both = one(a[...], b[:deep])
    return both[:rows] + (both[rows:] + one(a[:rows], b[deep:]))


def log_one_plus(t):
    series = t * (1.0 + t * (-0.5 + t * (1.0 / 3.0 + t * (-0.25 + t * 0.2))))
    return jnp.where(t < 0.03125, series, jnp.log(1.0 + t))


def gated(z, weight, diagonal=None):
    signed = z if diagonal is None else jnp.where(diagonal, -z, z)
    small = jnp.exp(-jnp.abs(signed))
    loss = jnp.maximum(signed, 0.0) + log_one_plus(small)
    slope = jnp.where(signed >= 0.0, 1.0, small) / (1.0 + small) * weight
    if diagonal is not None:
        slope = jnp.where(diagonal, -slope, slope)
    return loss, slope


def scale_of(raw):
    return lax.rsqrt(jnp.sum(raw * raw, axis=1, keepdims=True) + 1e-06)


def square(count):
    rows = lax.broadcasted_iota(jnp.int32, (count, count), 0)
    return rows == lax.broadcasted_iota(jnp.int32, (count, count), 1)


def temper_of(lt):
    return jnp.exp(jnp.full((1, 1), lt[0], F32))


def first_body(lt, bi, x_any, y_any, near_ref, w_ref, *refs):
    x_ref, xc_ref, y_ref, yc_ref, xs_ref, ys_ref, gx_ref, gy_ref, sum_ref, sem = refs
    copies = [
        pltpu.make_async_copy(x_any, x_ref, sem.at[0]),
        pltpu.make_async_copy(y_any, y_ref, sem.at[1]),
    ]
    for copy in copies:
        copy.start()
    temper = temper_of(lt)
    count = near_ref.shape[0]
    near = near_ref[...] * scale_of(near_ref[...])
    for copy, ref, scale_ref in zip(copies, (x_ref, y_ref), (xc_ref, yc_ref)):
        copy.wait()
        scale_ref[...] = scale_of(ref[...])
        ref[...] = ref[...] * scale_ref[...]
    xs_ref[...] = stacked(x_ref[...])
    ys_ref[...] = stacked(jnp.concatenate([y_ref[...], near], axis=0))
    rows = lax.broadcasted_iota(jnp.int32, (2 * count, count), 0)
    cols = lax.broadcasted_iota(jnp.int32, (2 * count, count), 1)
    z = temper * mm(ys_ref, xs_ref, NT) + bi[0]
    loss, slope = gated(z, w_ref[...] * temper, rows == cols)
    sum_ref[...] = jnp.sum(loss, axis=0, keepdims=True)
    gx_ref[...] = mm(stacked(slope.T), ys_ref, NN)
    gy_ref[...] = mm(stacked(slope), xs_ref, NN)


def second_body(others, lt, bi, *refs):
    raw_refs, refs = refs[:others], refs[others:]
    w_refs, refs = refs[:others], refs[others:]
    xs_ref, ys_ref, all_ref, refs = *refs[:3], refs[3:]
    gp_refs, refs = refs[:others], refs[others:]
    sump_refs, slope_refs = refs[:others], refs[others:]
    temper = temper_of(lt)
    count = raw_refs[0].shape[0]
    deep = (others + 1) * count
    eye = square(count)
    all_ref[:count] = xs_ref[:count]
    all_ref[deep : deep + count] = xs_ref[count:]
    for s in range(others):
        raw = raw_refs[s][...]
        px = stacked(raw * scale_of(raw))
        here = (s + 1) * count
        all_ref[here : here + count] = px[:count]
        all_ref[deep + here : deep + here + count] = px[count:]
        z = temper * mm(px, ys_ref, NT) + bi[0]
        weight = jnp.sum(jnp.where(eye, w_refs[s][...], 0.0), axis=1, keepdims=True)
        loss, slope = gated(z, weight * temper)
        sums = jnp.sum(loss, axis=1, keepdims=True)
        sump_refs[s][...] = jnp.sum(jnp.where(eye, sums, 0.0), axis=0, keepdims=True)
        slope_refs[s][...] = slope
        gp_refs[s][...] = mm(stacked(slope), ys_ref, NN)


def third_body(others, lt, bi, *refs):
    members = others + 1
    far_ref, refs = refs[0], refs[1:]
    w_refs, refs = refs[:members], refs[members:]
    all_ref, refs = refs[0], refs[1:]
    gp_in, refs = refs[:others], refs[others:]
    sum_in, refs = refs[:members], refs[members:]
    gfar_ref, refs = refs[0], refs[1:]
    gp_refs, refs = refs[:others], refs[others:]
    sum_refs, refs = refs[:members], refs[members:]
    fs_ref, slope_ref = refs
    temper = temper_of(lt)
    count = far_ref.shape[0]
    fs_ref[...] = stacked(far_ref[...])
    scale = scale_of(far_ref[...])
    z = (temper * scale) * mm(fs_ref, all_ref, NT) + bi[0]
    weight = jnp.concatenate([w[...] for w in w_refs], axis=1) * temper
    loss, slope = gated(z, weight)
    gfar_ref[...] = mm(stacked(slope), all_ref, NN)
    slope = slope * scale
    sums = jnp.sum(loss, axis=0, keepdims=True)
    for s in range(members):
        part = slice(s * count, (s + 1) * count)
        sum_refs[s][...] = sum_in[s][...] + sums[:, part]
        if s == 0:
            slope_ref[...] = slope[:, part]
        else:
            gp_refs[s - 1][...] = gp_in[s - 1][...] + mm(stacked(slope[:, part].T), fs_ref, NN)


def fourth_body(others, gx_in, gy_in, slope_ref, fs_ref, all_ref, *refs):
    slopes, (gx_ref, gown_ref, gnear_ref) = refs[:others], refs[others:]
    count = gx_in.shape[0]
    deep = (others + 1) * count
    gy = gy_in[...]
    for s in range(others):
        here = (s + 1) * count
        px = jnp.concatenate(
            [all_ref[here : here + count], all_ref[deep + here : deep + here + count]], axis=0
        )
        gy = gy + mm(stacked(slopes[s][...].T), px, NN)
    gown_ref[...] = gy[:count]
    gnear_ref[...] = gy[count:]
    gx_ref[...] = gx_in[...] + mm(stacked(slope_ref[...].T), fs_ref, NN)


def last_body(terms, lines, pairs, unit_ref, scale_ref, *refs):
    grads, refs = refs[:terms], refs[terms:]
    sums, refs = refs[:lines], refs[lines:]
    if lines:
        out_ref, loss_ref, held, sem, line = refs
    else:
        out_ref, held, sem = refs
    rows = unit_ref.shape[0] // CHUNKS
    copies = []
    if lines:
        total = sums[0][...]
        for r in sums[1:]:
            total = total + r[...]
        line[...] = total / pairs
        copies.append(pltpu.make_async_copy(line, loss_ref, sem.at[CHUNKS]))
        copies[-1].start()
    for c in range(CHUNKS):
        here = pl.ds(c * rows, rows)
        grad = grads[0][here, :]
        for r in grads[1:]:
            grad = grad + r[here, :]
        unit = unit_ref[here, :]
        inner = jnp.sum(unit * grad, axis=1, keepdims=True)
        held[here, :] = scale_ref[here, :] * (grad - unit * inner)
        copies.append(pltpu.make_async_copy(held.at[here, :], out_ref.at[here, :], sem.at[c]))
        copies[-1].start()
    for copy in copies:
        copy.wait()


def shape(*dims, kind=F32):
    return jax.ShapeDtypeStruct(dims, kind)


PARAMS = pltpu.CompilerParams(vmem_limit_bytes=16 * 1024 * 1024)


def in_hbm(args):
    return [pltpu.with_memory_space_constraint(a, pltpu.HBM) for a in args]


def in_vmem(args):
    return [pltpu.with_memory_space_constraint(a, pltpu.VMEM) for a in args]


def call(body, outs, scalars, *args, scratch=(), anywhere=0):
    return pl.pallas_call(
        body,
        out_shape=[pltpu.VMEM(o.shape, o.dtype) for o in outs],
        in_specs=[SMEM] * len(scalars) + [HBM] * anywhere + [VMEM] * (len(args) - anywhere),
        out_specs=[VMEM] * len(outs),
        scratch_shapes=list(scratch),
        compiler_params=PARAMS,
    )(*scalars, *in_hbm(args[:anywhere]), *in_vmem(args[anywhere:]))


def finish(unit, scale, grads, sums=(), pairs=None):
    full = shape(*unit.shape)
    line = shape(1, unit.shape[0])
    args = [unit, scale, *grads, *sums]
    extra = [pltpu.VMEM(line.shape, F32)] if sums else []
    outs = [full, line] if sums else [full]
    return pl.pallas_call(
        functools.partial(last_body, len(grads), len(sums), pairs),
        out_shape=outs,
        in_specs=[VMEM] * len(args),
        out_specs=[HBM] * len(outs),
        scratch_shapes=[
            pltpu.VMEM(full.shape, F32),
            pltpu.SemaphoreType.DMA((CHUNKS + 1,)),
            *extra,
        ],
        compiler_params=PARAMS,
    )(*in_vmem(args))


def body(images, texts, log_temp, bias, row_weight):
    members = lax.axis_size("grp")
    others = members - 1
    count, width = images.shape
    weight = row_weight.reshape(1, count)
    scalars = (log_temp, bias)
    raws = [shifted(images, "grp", -s) for s in range(1, members)]
    far = swapped(texts, "blk", False)
    near = swapped(texts, "blk", True)
    weights = [weight] + [shifted(weight, "grp", -s) for s in range(1, members)]
    full = shape(count, width)
    line = shape(1, count)
    stack = shape(2 * count, width, kind=BF)
    unit_x, scale_x, unit_y, scale_y, xs, ys, gx, gy, sums = call(
        first_body,
        [
            full,
            shape(count, 1),
            full,
            shape(count, 1),
            stack,
            shape(4 * count, width, kind=BF),
            full,
            shape(2 * count, width),
            line,
        ],
        scalars,
        images,
        texts,
        near,
        weight,
        scratch=[pltpu.SemaphoreType.DMA((2,))],
        anywhere=2,
    )
    outs = call(
        functools.partial(second_body, others),
        [shape(2 * members * count, width, kind=BF)]
        + [full] * others
        + [line] * others
        + [shape(count, 2 * count)] * others,
        scalars,
        *raws,
        *weights[1:],
        xs,
        ys,
    )
    everyone, outs = outs[0], outs[1:]
    gp, outs = outs[:others], outs[others:]
    sump, slopes = outs[:others], outs[others:]
    outs = call(
        functools.partial(third_body, others),
        [full] + [full] * others + [line] * members + [stack, shape(count, count)],
        scalars,
        far,
        *weights,
        everyone,
        *gp,
        sums,
        *sump,
    )
    g_far, outs = outs[0], outs[1:]
    gp, outs = outs[:others], outs[others:]
    sums, (fs, slope) = outs[:members], outs[members:]
    back_far = swapped(g_far, "blk", False)
    back_x = [shifted(gp[s - 1], "grp", s) for s in range(1, members)]
    back_sum = [shifted(sums[s], "grp", s) for s in range(1, members)]
    gx, g_own, g_near = call(
        functools.partial(fourth_body, others),
        [full] * 3,
        (),
        gx,
        gy,
        slope,
        fs,
        everyone,
        *slopes,
    )
    back_near = swapped(g_near, "blk", True)
    pairs = 3.0 * members * count
    grad_x, row_loss = finish(unit_x, scale_x, [gx, *back_x], [sums[0], *back_sum], pairs)
    (grad_y,) = finish(unit_y, scale_y, [g_own, back_near, back_far])
    return (row_loss.reshape(count), grad_x, grad_y)


def solution(mesh):
    placed = (P(("blk", "grp"), None), P(("blk", "grp"), None), P(), P(), P(("blk", "grp")))
    return jax.shard_map(
        body,
        mesh=mesh,
        in_specs=placed,
        out_specs=(P(("blk", "grp")), P(("blk", "grp"), None), P(("blk", "grp"), None)),
        check_vma=False,
    )
```

```python
import functools

import jax
import jax.numpy as jnp
from jax import lax
from jax.experimental import pallas as pl
from jax.experimental.pallas import tpu as pltpu
from jax.sharding import PartitionSpec as P


BF = jnp.bfloat16
F32 = jnp.float32
VMEM = pl.BlockSpec(memory_space=pltpu.VMEM)
SMEM = pl.BlockSpec(memory_space=pltpu.SMEM)
HBM = pl.BlockSpec(memory_space=pltpu.HBM)
CHUNKS = 4
NT = ((1,), (1,))
NN = ((1,), (0,))


def exchanged(x, axis, pairs):
    return lax.ppermute(x, axis, pairs + [(b, a) for (a, b) in pairs])


def far_pairs(length):
    pairs = [(i, (i + 1) % length) for i in range(1, length, 2)]
    return [pairs[0::2], pairs[1::2]]


def shifted(x, axis, by):
    length = lax.axis_size(axis)
    return lax.ppermute(x, axis, [(i, (i + by) % length) for i in range(length)])


def stacked(v):
    high = v.astype(BF)
    return jnp.concatenate([high, (v - high.astype(F32)).astype(BF)], axis=0)


def mm(a, b, dims):
    rows = a.shape[0] // 2
    deep = b.shape[0] // 2

    def one(p, q):
        return lax.dot_general(p, q, (dims, ((), ())), preferred_element_type=F32)

    both = one(a[...], b[:deep])
    return both[:rows] + (both[rows:] + one(a[:rows], b[deep:]))


def log_one_plus(t):
    series = t * (1.0 + t * (-0.5 + t * (1.0 / 3.0 + t * (-0.25 + t * 0.2))))
    return jnp.where(t < 0.03125, series, jnp.log(1.0 + t))


def gated(z, weight, diagonal=None):
    signed = z if diagonal is None else jnp.where(diagonal, -z, z)
    small = jnp.exp(-jnp.abs(signed))
    loss = jnp.maximum(signed, 0.0) + log_one_plus(small)
    slope = jnp.where(signed >= 0.0, 1.0, small) / (1.0 + small) * weight
    if diagonal is not None:
        slope = jnp.where(diagonal, -slope, slope)
    return loss, slope


def scale_of(raw):
    return lax.rsqrt(jnp.sum(raw * raw, axis=1, keepdims=True) + 1e-06)


def square(count):
    rows = lax.broadcasted_iota(jnp.int32, (count, count), 0)
    return rows == lax.broadcasted_iota(jnp.int32, (count, count), 1)


def temper_of(lt):
    return jnp.exp(jnp.full((1, 1), lt[0], F32))


def first_body(lt, bi, x_any, y_any, near_ref, w_ref, *refs):
    x_ref, xc_ref, y_ref, yc_ref, xs_ref, ys_ref, gx_ref, gy_ref, sum_ref, sem = refs
    copies = [
        pltpu.make_async_copy(x_any, x_ref, sem.at[0]),
        pltpu.make_async_copy(y_any, y_ref, sem.at[1]),
    ]
    for copy in copies:
        copy.start()
    temper = temper_of(lt)
    count = near_ref.shape[0]
    near = near_ref[...] * scale_of(near_ref[...])
    for copy, ref, scale_ref in zip(copies, (x_ref, y_ref), (xc_ref, yc_ref)):
        copy.wait()
        scale_ref[...] = scale_of(ref[...])
        ref[...] = ref[...] * scale_ref[...]
    xs_ref[...] = stacked(x_ref[...])
    ys_ref[...] = stacked(jnp.concatenate([y_ref[...], near], axis=0))
    rows = lax.broadcasted_iota(jnp.int32, (2 * count, count), 0)
    cols = lax.broadcasted_iota(jnp.int32, (2 * count, count), 1)
    z = temper * mm(ys_ref, xs_ref, NT) + bi[0]
    loss, slope = gated(z, w_ref[...] * temper, rows == cols)
    sum_ref[...] = jnp.sum(loss, axis=0, keepdims=True)
    gx_ref[...] = mm(stacked(slope.T), ys_ref, NN)
    gy_ref[...] = mm(stacked(slope), xs_ref, NN)


def second_body(others, lt, bi, *refs):
    raw_refs, refs = refs[:others], refs[others:]
    w_refs, refs = refs[:others], refs[others:]
    xs_ref, ys_ref, all_ref, refs = *refs[:3], refs[3:]
    gp_refs, refs = refs[:others], refs[others:]
    sump_refs, slope_refs = refs[:others], refs[others:]
    temper = temper_of(lt)
    count = raw_refs[0].shape[0]
    deep = (others + 1) * count
    eye = square(count)
    all_ref[:count] = xs_ref[:count]
    all_ref[deep : deep + count] = xs_ref[count:]
    for s in range(others):
        raw = raw_refs[s][...]
        px = stacked(raw * scale_of(raw))
        here = (s + 1) * count
        all_ref[here : here + count] = px[:count]
        all_ref[deep + here : deep + here + count] = px[count:]
        z = temper * mm(px, ys_ref, NT) + bi[0]
        weight = jnp.sum(jnp.where(eye, w_refs[s][...], 0.0), axis=1, keepdims=True)
        loss, slope = gated(z, weight * temper)
        sums = jnp.sum(loss, axis=1, keepdims=True)
        sump_refs[s][...] = jnp.sum(jnp.where(eye, sums, 0.0), axis=0, keepdims=True)
        slope_refs[s][...] = slope
        gp_refs[s][...] = mm(stacked(slope), ys_ref, NN)


def third_body(others, lt, bi, *refs):
    members = others + 1
    early_ref, late_ref, refs = *refs[:2], refs[2:]
    w_refs, refs = refs[:members], refs[members:]
    all_ref, refs = refs[0], refs[1:]
    gp_in, refs = refs[:others], refs[others:]
    sum_in, refs = refs[:members], refs[members:]
    gfar_ref, refs = refs[0], refs[1:]
    gp_refs, refs = refs[:others], refs[others:]
    sum_refs, refs = refs[:members], refs[members:]
    fs_ref, slope_ref = refs
    temper = temper_of(lt)
    count = early_ref.shape[0]
    far = early_ref[...] + late_ref[...]
    fs_ref[...] = stacked(far)
    scale = scale_of(far)
    z = (temper * scale) * mm(fs_ref, all_ref, NT) + bi[0]
    weight = jnp.concatenate([w[...] for w in w_refs], axis=1) * temper
    loss, slope = gated(z, weight)
    gfar_ref[...] = mm(stacked(slope), all_ref, NN)
    slope = slope * scale
    sums = jnp.sum(loss, axis=0, keepdims=True)
    for s in range(members):
        part = slice(s * count, (s + 1) * count)
        sum_refs[s][...] = sum_in[s][...] + sums[:, part]
        if s == 0:
            slope_ref[...] = slope[:, part]
        else:
            gp_refs[s - 1][...] = gp_in[s - 1][...] + mm(stacked(slope[:, part].T), fs_ref, NN)


def fourth_body(others, gx_in, gy_in, slope_ref, fs_ref, all_ref, *refs):
    slopes, (gx_ref, gown_ref, gnear_ref) = refs[:others], refs[others:]
    count = gx_in.shape[0]
    deep = (others + 1) * count
    gy = gy_in[...]
    for s in range(others):
        here = (s + 1) * count
        px = jnp.concatenate(
            [all_ref[here : here + count], all_ref[deep + here : deep + here + count]], axis=0
        )
        gy = gy + mm(stacked(slopes[s][...].T), px, NN)
    gown_ref[...] = gy[:count]
    gnear_ref[...] = gy[count:]
    gx_ref[...] = gx_in[...] + mm(stacked(slope_ref[...].T), fs_ref, NN)


def last_body(terms, lines, pairs, unit_ref, scale_ref, *refs):
    grads, refs = refs[:terms], refs[terms:]
    sums, refs = refs[:lines], refs[lines:]
    if lines:
        out_ref, loss_ref, held, sem, line = refs
    else:
        out_ref, held, sem = refs
    rows = unit_ref.shape[0] // CHUNKS
    copies = []
    if lines:
        total = sums[0][...]
        for r in sums[1:]:
            total = total + r[...]
        line[...] = total / pairs
        copies.append(pltpu.make_async_copy(line, loss_ref, sem.at[CHUNKS]))
        copies[-1].start()
    for c in range(CHUNKS):
        here = pl.ds(c * rows, rows)
        grad = grads[0][here, :]
        for r in grads[1:]:
            grad = grad + r[here, :]
        unit = unit_ref[here, :]
        inner = jnp.sum(unit * grad, axis=1, keepdims=True)
        held[here, :] = scale_ref[here, :] * (grad - unit * inner)
        copies.append(pltpu.make_async_copy(held.at[here, :], out_ref.at[here, :], sem.at[c]))
        copies[-1].start()
    for copy in copies:
        copy.wait()


def shape(*dims, kind=F32):
    return jax.ShapeDtypeStruct(dims, kind)


PARAMS = pltpu.CompilerParams(vmem_limit_bytes=16 * 1024 * 1024)


def in_hbm(args):
    return [pltpu.with_memory_space_constraint(a, pltpu.HBM) for a in args]


def in_vmem(args):
    return [pltpu.with_memory_space_constraint(a, pltpu.VMEM) for a in args]


def call(body, outs, scalars, *args, scratch=(), anywhere=0):
    return pl.pallas_call(
        body,
        out_shape=[pltpu.VMEM(o.shape, o.dtype) for o in outs],
        in_specs=[SMEM] * len(scalars) + [HBM] * anywhere + [VMEM] * (len(args) - anywhere),
        out_specs=[VMEM] * len(outs),
        scratch_shapes=list(scratch),
        compiler_params=PARAMS,
    )(*scalars, *in_hbm(args[:anywhere]), *in_vmem(args[anywhere:]))


def finish(unit, scale, grads, sums=(), pairs=None):
    full = shape(*unit.shape)
    line = shape(1, unit.shape[0])
    args = [unit, scale, *grads, *sums]
    extra = [pltpu.VMEM(line.shape, F32)] if sums else []
    outs = [full, line] if sums else [full]
    return pl.pallas_call(
        functools.partial(last_body, len(grads), len(sums), pairs),
        out_shape=outs,
        in_specs=[VMEM] * len(args),
        out_specs=[HBM] * len(outs),
        scratch_shapes=[
            pltpu.VMEM(full.shape, F32),
            pltpu.SemaphoreType.DMA((CHUNKS + 1,)),
            *extra,
        ],
        compiler_params=PARAMS,
    )(*in_vmem(args))


def body(images, texts, log_temp, bias, row_weight):
    members = lax.axis_size("grp")
    others = members - 1
    count, width = images.shape
    weight = row_weight.reshape(1, count)
    scalars = (log_temp, bias)
    length = lax.axis_size("blk")
    near_pairs = [(i, i + 1) for i in range(0, length, 2)]
    early, late = far_pairs(length)
    far_early = exchanged(texts, "blk", early)
    raws = [shifted(images, "grp", -s) for s in range(1, members)]
    far_late = exchanged(texts, "blk", late)
    near = exchanged(texts, "blk", near_pairs)
    weights = [weight] + [shifted(weight, "grp", -s) for s in range(1, members)]
    full = shape(count, width)
    line = shape(1, count)
    stack = shape(2 * count, width, kind=BF)
    unit_x, scale_x, unit_y, scale_y, xs, ys, gx, gy, sums = call(
        first_body,
        [
            full,
            shape(count, 1),
            full,
            shape(count, 1),
            stack,
            shape(4 * count, width, kind=BF),
            full,
            shape(2 * count, width),
            line,
        ],
        scalars,
        images,
        texts,
        near,
        weight,
        scratch=[pltpu.SemaphoreType.DMA((2,))],
        anywhere=2,
    )
    outs = call(
        functools.partial(second_body, others),
        [shape(2 * members * count, width, kind=BF)]
        + [full] * others
        + [line] * others
        + [shape(count, 2 * count)] * others,
        scalars,
        *raws,
        *weights[1:],
        xs,
        ys,
    )
    everyone, outs = outs[0], outs[1:]
    gp, outs = outs[:others], outs[others:]
    sump, slopes = outs[:others], outs[others:]
    outs = call(
        functools.partial(third_body, others),
        [full] + [full] * others + [line] * members + [stack, shape(count, count)],
        scalars,
        far_early,
        far_late,
        *weights,
        everyone,
        *gp,
        sums,
        *sump,
    )
    g_far, outs = outs[0], outs[1:]
    gp, outs = outs[:others], outs[others:]
    sums, (fs, slope) = outs[:members], outs[members:]
    back_early = exchanged(g_far, "blk", early)
    back_x = [shifted(gp[s - 1], "grp", s) for s in range(1, members)]
    back_late = exchanged(g_far, "blk", late)
    back_sum = [shifted(sums[s], "grp", s) for s in range(1, members)]
    gx, g_own, g_near = call(
        functools.partial(fourth_body, others),
        [full] * 3,
        (),
        gx,
        gy,
        slope,
        fs,
        everyone,
        *slopes,
    )
    back_near = exchanged(g_near, "blk", near_pairs)
    pairs = 3.0 * members * count
    grad_x, row_loss = finish(unit_x, scale_x, [gx, *back_x], [sums[0], *back_sum], pairs)
    (grad_y,) = finish(unit_y, scale_y, [g_own, back_near, back_early, back_late])
    return (row_loss.reshape(count), grad_x, grad_y)


def solution(mesh):
    placed = (P(("blk", "grp"), None), P(("blk", "grp"), None), P(), P(), P(("blk", "grp")))
    return jax.shard_map(
        body,
        mesh=mesh,
        in_specs=placed,
        out_specs=(P(("blk", "grp")), P(("blk", "grp"), None), P(("blk", "grp"), None)),
        check_vma=False,
    )
```

```python
import functools

import jax
import jax.numpy as jnp
from jax import lax
from jax.experimental import pallas as pl
from jax.experimental.pallas import tpu as pltpu
from jax.sharding import PartitionSpec as P


BF = jnp.bfloat16
F32 = jnp.float32
VMEM = pl.BlockSpec(memory_space=pltpu.VMEM)
SMEM = pl.BlockSpec(memory_space=pltpu.SMEM)
HBM = pl.BlockSpec(memory_space=pltpu.HBM)
CHUNKS = 4
NT = ((1,), (1,))
NN = ((1,), (0,))


def exchanged(x, axis, pairs):
    paired = {i for pair in pairs for i in pair}
    alone = [(i, i) for i in range(lax.axis_size(axis)) if i not in paired]
    return lax.ppermute(x, axis, pairs + [(b, a) for (a, b) in pairs] + alone)


def shifted(x, axis, by):
    length = lax.axis_size(axis)
    return lax.ppermute(x, axis, [(i, (i + by) % length) for i in range(length)])


def stacked(v):
    high = v.astype(BF)
    return jnp.concatenate([high, (v - high.astype(F32)).astype(BF)], axis=0)


def mm(a, b, dims):
    rows = a.shape[0] // 2
    deep = b.shape[0] // 2

    def one(p, q):
        return lax.dot_general(p, q, (dims, ((), ())), preferred_element_type=F32)

    both = one(a[...], b[:deep])
    return both[:rows] + (both[rows:] + one(a[:rows], b[deep:]))


def log_one_plus(t):
    series = t * (1.0 + t * (-0.5 + t * (1.0 / 3.0 + t * (-0.25 + t * 0.2))))
    return jnp.where(t < 0.03125, series, jnp.log(1.0 + t))


def gated(z, weight, diagonal=None):
    signed = z if diagonal is None else jnp.where(diagonal, -z, z)
    small = jnp.exp(-jnp.abs(signed))
    loss = jnp.maximum(signed, 0.0) + log_one_plus(small)
    slope = jnp.where(signed >= 0.0, 1.0, small) / (1.0 + small) * weight
    if diagonal is not None:
        slope = jnp.where(diagonal, -slope, slope)
    return loss, slope


def scale_of(raw):
    return lax.rsqrt(jnp.sum(raw * raw, axis=1, keepdims=True) + 1e-06)


def square(count):
    rows = lax.broadcasted_iota(jnp.int32, (count, count), 0)
    return rows == lax.broadcasted_iota(jnp.int32, (count, count), 1)


def temper_of(lt):
    return jnp.exp(jnp.full((1, 1), lt[0], F32))


def first_body(lt, bi, x_any, y_any, near_ref, w_ref, *refs):
    x_ref, xc_ref, y_ref, yc_ref, xs_ref, ys_ref, gx_ref, gy_ref, sum_ref, sem = refs
    copies = [
        pltpu.make_async_copy(x_any, x_ref, sem.at[0]),
        pltpu.make_async_copy(y_any, y_ref, sem.at[1]),
    ]
    for copy in copies:
        copy.start()
    temper = temper_of(lt)
    count = near_ref.shape[0]
    near = near_ref[...] * scale_of(near_ref[...])
    for copy, ref, scale_ref in zip(copies, (x_ref, y_ref), (xc_ref, yc_ref)):
        copy.wait()
        scale_ref[...] = scale_of(ref[...])
        ref[...] = ref[...] * scale_ref[...]
    xs_ref[...] = stacked(x_ref[...])
    ys_ref[...] = stacked(jnp.concatenate([y_ref[...], near], axis=0))
    rows = lax.broadcasted_iota(jnp.int32, (2 * count, count), 0)
    cols = lax.broadcasted_iota(jnp.int32, (2 * count, count), 1)
    z = temper * mm(ys_ref, xs_ref, NT) + bi[0]
    loss, slope = gated(z, w_ref[...] * temper, rows == cols)
    sum_ref[...] = jnp.sum(loss, axis=0, keepdims=True)
    gx_ref[...] = mm(stacked(slope.T), ys_ref, NN)
    gy_ref[...] = mm(stacked(slope), xs_ref, NN)


def second_body(others, lt, bi, *refs):
    raw_refs, refs = refs[:others], refs[others:]
    w_refs, refs = refs[:others], refs[others:]
    xs_ref, ys_ref, all_ref, refs = *refs[:3], refs[3:]
    gp_refs, refs = refs[:others], refs[others:]
    sump_refs, slope_refs = refs[:others], refs[others:]
    temper = temper_of(lt)
    count = raw_refs[0].shape[0]
    deep = (others + 1) * count
    eye = square(count)
    all_ref[:count] = xs_ref[:count]
    all_ref[deep : deep + count] = xs_ref[count:]
    for s in range(others):
        raw = raw_refs[s][...]
        px = stacked(raw * scale_of(raw))
        here = (s + 1) * count
        all_ref[here : here + count] = px[:count]
        all_ref[deep + here : deep + here + count] = px[count:]
        z = temper * mm(px, ys_ref, NT) + bi[0]
        weight = jnp.sum(jnp.where(eye, w_refs[s][...], 0.0), axis=1, keepdims=True)
        loss, slope = gated(z, weight * temper)
        sums = jnp.sum(loss, axis=1, keepdims=True)
        sump_refs[s][...] = jnp.sum(jnp.where(eye, sums, 0.0), axis=0, keepdims=True)
        slope_refs[s][...] = slope
        gp_refs[s][...] = mm(stacked(slope), ys_ref, NN)


def third_body(others, lt, bi, at_end, *refs):
    members = others + 1
    far_ref, end_ref, refs = *refs[:2], refs[2:]
    w_refs, refs = refs[:members], refs[members:]
    all_ref, refs = refs[0], refs[1:]
    gp_in, refs = refs[:others], refs[others:]
    sum_in, refs = refs[:members], refs[members:]
    gfar_ref, refs = refs[0], refs[1:]
    gp_refs, refs = refs[:others], refs[others:]
    sum_refs, refs = refs[:members], refs[members:]
    fs_ref, slope_ref = refs
    temper = temper_of(lt)
    count = far_ref.shape[0]
    far = jnp.where(at_end[0] == 1, end_ref[...], far_ref[...])
    fs_ref[...] = stacked(far)
    scale = scale_of(far)
    z = (temper * scale) * mm(fs_ref, all_ref, NT) + bi[0]
    weight = jnp.concatenate([w[...] for w in w_refs], axis=1) * temper
    loss, slope = gated(z, weight)
    gfar_ref[...] = mm(stacked(slope), all_ref, NN)
    slope = slope * scale
    sums = jnp.sum(loss, axis=0, keepdims=True)
    for s in range(members):
        part = slice(s * count, (s + 1) * count)
        sum_refs[s][...] = sum_in[s][...] + sums[:, part]
        if s == 0:
            slope_ref[...] = slope[:, part]
        else:
            gp_refs[s - 1][...] = gp_in[s - 1][...] + mm(stacked(slope[:, part].T), fs_ref, NN)


def fourth_body(others, gx_in, gy_in, slope_ref, fs_ref, all_ref, *refs):
    slopes, (gx_ref, gown_ref, gnear_ref) = refs[:others], refs[others:]
    count = gx_in.shape[0]
    deep = (others + 1) * count
    gy = gy_in[...]
    for s in range(others):
        here = (s + 1) * count
        px = jnp.concatenate(
            [all_ref[here : here + count], all_ref[deep + here : deep + here + count]], axis=0
        )
        gy = gy + mm(stacked(slopes[s][...].T), px, NN)
    gown_ref[...] = gy[:count]
    gnear_ref[...] = gy[count:]
    gx_ref[...] = gx_in[...] + mm(stacked(slope_ref[...].T), fs_ref, NN)


def last_body(others, pairs, at_end, *refs):
    (unit_x, scale_x, own_x), refs = refs[:3], refs[3:]
    back_x, refs = refs[:others], refs[others:]
    (unit_y, scale_y, own_y, near_y, far_y, end_y), refs = refs[:6], refs[6:]
    sums, refs = refs[: others + 1], refs[others + 1 :]
    x_out, y_out, loss_out, held, line, sem = refs
    rows = unit_x.shape[0] // CHUNKS
    copies = []

    def send(source, target):
        copies.append(pltpu.make_async_copy(source, target, sem.at[len(copies)]))
        copies[-1].start()

    def through(k, here, unit, scale, grad, out_ref):
        inner = jnp.sum(unit * grad, axis=1, keepdims=True)
        held[k, here, :] = scale * (grad - unit * inner)
        send(held.at[k, here, :], out_ref.at[here, :])

    total = sums[0][...]
    for r in sums[1:]:
        total = total + r[...]
    line[...] = total / pairs
    send(line, loss_out)
    for c in range(CHUNKS):
        here = pl.ds(c * rows, rows)
        grad = own_x[here, :]
        for r in back_x:
            grad = grad + r[here, :]
        through(0, here, unit_x[here, :], scale_x[here, :], grad, x_out)
    for c in range(CHUNKS):
        here = pl.ds(c * rows, rows)
        grad = jnp.where(at_end[0] == 1, end_y[here, :], far_y[here, :])
        grad = own_y[here, :] + near_y[here, :] + grad
        through(1, here, unit_y[here, :], scale_y[here, :], grad, y_out)
    for copy in copies:
        copy.wait()


def shape(*dims, kind=F32):
    return jax.ShapeDtypeStruct(dims, kind)


PARAMS = pltpu.CompilerParams(vmem_limit_bytes=16 * 1024 * 1024)


def in_hbm(args):
    return [pltpu.with_memory_space_constraint(a, pltpu.HBM) for a in args]


def in_vmem(args):
    return [pltpu.with_memory_space_constraint(a, pltpu.VMEM) for a in args]


def call(body, outs, scalars, *args, scratch=(), anywhere=0):
    return pl.pallas_call(
        body,
        out_shape=[pltpu.VMEM(o.shape, o.dtype) for o in outs],
        in_specs=[SMEM] * len(scalars) + [HBM] * anywhere + [VMEM] * (len(args) - anywhere),
        out_specs=[VMEM] * len(outs),
        scratch_shapes=list(scratch),
        compiler_params=PARAMS,
    )(*scalars, *in_hbm(args[:anywhere]), *in_vmem(args[anywhere:]))


def finish(others, pairs, at_end, *args):
    full = shape(*args[0].shape)
    line = shape(1, full.shape[0])
    return pl.pallas_call(
        functools.partial(last_body, others, pairs),
        out_shape=[full, full, line],
        in_specs=[SMEM] + [VMEM] * len(args),
        out_specs=[HBM] * 3,
        scratch_shapes=[
            pltpu.VMEM((2, *full.shape), F32),
            pltpu.VMEM(line.shape, F32),
            pltpu.SemaphoreType.DMA((2 * CHUNKS + 1,)),
        ],
        compiler_params=PARAMS,
    )(at_end, *in_vmem(args))


def body(images, texts, log_temp, bias, row_weight):
    members = lax.axis_size("grp")
    others = members - 1
    count, width = images.shape
    weight = row_weight.reshape(1, count)
    scalars = (log_temp, bias)
    length = lax.axis_size("blk")
    near_pairs = [(i, i + 1) for i in range(0, length, 2)]
    far_pairs = [(i, i + 1) for i in range(1, length - 1, 2)]
    ends = [(length - 1, 0)]
    place = lax.axis_index("blk")
    at_end = jnp.where((place == 0) | (place == length - 1), 1, 0).astype(jnp.int32).reshape(1)
    far = exchanged(texts, "blk", far_pairs)
    raws = [shifted(images, "grp", -s) for s in range(1, members)]
    far_end = exchanged(texts, "blk", ends)
    near = exchanged(texts, "blk", near_pairs)
    weights = [weight] + [shifted(weight, "grp", -s) for s in range(1, members)]
    full = shape(count, width)
    line = shape(1, count)
    stack = shape(2 * count, width, kind=BF)
    unit_x, scale_x, unit_y, scale_y, xs, ys, gx, gy, sums = call(
        first_body,
        [
            full,
            shape(count, 1),
            full,
            shape(count, 1),
            stack,
            shape(4 * count, width, kind=BF),
            full,
            shape(2 * count, width),
            line,
        ],
        scalars,
        images,
        texts,
        near,
        weight,
        scratch=[pltpu.SemaphoreType.DMA((2,))],
        anywhere=2,
    )
    outs = call(
        functools.partial(second_body, others),
        [shape(2 * members * count, width, kind=BF)]
        + [full] * others
        + [line] * others
        + [shape(count, 2 * count)] * others,
        scalars,
        *raws,
        *weights[1:],
        xs,
        ys,
    )
    everyone, outs = outs[0], outs[1:]
    gp, outs = outs[:others], outs[others:]
    sump, slopes = outs[:others], outs[others:]
    outs = call(
        functools.partial(third_body, others),
        [full] + [full] * others + [line] * members + [stack, shape(count, count)],
        (*scalars, at_end),
        far,
        far_end,
        *weights,
        everyone,
        *gp,
        sums,
        *sump,
    )
    g_far, outs = outs[0], outs[1:]
    gp, outs = outs[:others], outs[others:]
    sums, (fs, slope) = outs[:members], outs[members:]
    back_far = exchanged(g_far, "blk", far_pairs)
    back_x = [shifted(gp[s - 1], "grp", s) for s in range(1, members)]
    back_end = exchanged(g_far, "blk", ends)
    back_sum = [shifted(sums[s], "grp", s) for s in range(1, members)]
    gx, g_own, g_near = call(
        functools.partial(fourth_body, others),
        [full] * 3,
        (),
        gx,
        gy,
        slope,
        fs,
        everyone,
        *slopes,
    )
    back_near = exchanged(g_near, "blk", near_pairs)
    grad_x, grad_y, row_loss = finish(
        others,
        3.0 * members * count,
        at_end,
        unit_x,
        scale_x,
        gx,
        *back_x,
        unit_y,
        scale_y,
        g_own,
        back_near,
        back_far,
        back_end,
        sums[0],
        *back_sum,
    )
    return (row_loss.reshape(count), grad_x, grad_y)


def solution(mesh):
    placed = (P(("blk", "grp"), None), P(("blk", "grp"), None), P(), P(), P(("blk", "grp")))
    return jax.shard_map(
        body,
        mesh=mesh,
        in_specs=placed,
        out_specs=(P(("blk", "grp")), P(("blk", "grp"), None), P(("blk", "grp"), None)),
        check_vma=False,
    )
```

```python
import functools

import jax
import jax.numpy as jnp
from jax import lax
from jax.experimental import pallas as pl
from jax.experimental.pallas import tpu as pltpu
from jax.sharding import PartitionSpec as P


BF = jnp.bfloat16
F32 = jnp.float32
VMEM = pl.BlockSpec(memory_space=pltpu.VMEM)
SMEM = pl.BlockSpec(memory_space=pltpu.SMEM)
HBM = pl.BlockSpec(memory_space=pltpu.HBM)
CHUNKS = 4
NT = ((1,), (1,))
NN = ((1,), (0,))


def exchanged(x, axis, pairs):
    return lax.ppermute(x, axis, pairs + [(b, a) for (a, b) in pairs])


def shifted(x, axis, by):
    length = lax.axis_size(axis)
    return lax.ppermute(x, axis, [(i, (i + by) % length) for i in range(length)])


def stacked(v):
    high = v.astype(BF)
    return jnp.concatenate([high, (v - high.astype(F32)).astype(BF)], axis=0)


def mm(a, b, dims):
    rows = a.shape[0] // 2
    deep = b.shape[0] // 2

    def one(p, q):
        return lax.dot_general(p, q, (dims, ((), ())), preferred_element_type=F32)

    both = one(a[...], b[:deep])
    return both[:rows] + (both[rows:] + one(a[:rows], b[deep:]))


def log_one_plus(t):
    series = t * (1.0 + t * (-0.5 + t * (1.0 / 3.0 + t * (-0.25 + t * 0.2))))
    return jnp.where(t < 0.03125, series, jnp.log(1.0 + t))


def gated(z, weight, diagonal=None):
    signed = z if diagonal is None else jnp.where(diagonal, -z, z)
    small = jnp.exp(-jnp.abs(signed))
    loss = jnp.maximum(signed, 0.0) + log_one_plus(small)
    slope = jnp.where(signed >= 0.0, 1.0, small) / (1.0 + small) * weight
    if diagonal is not None:
        slope = jnp.where(diagonal, -slope, slope)
    return loss, slope


def scale_of(raw):
    return lax.rsqrt(jnp.sum(raw * raw, axis=1, keepdims=True) + 1e-06)


def square(count):
    rows = lax.broadcasted_iota(jnp.int32, (count, count), 0)
    return rows == lax.broadcasted_iota(jnp.int32, (count, count), 1)


def scalars_of(tb_ref):
    return tb_ref[0:1, 0:1], tb_ref[1:2, 0:1]


def first_body(lt, bi, x_any, y_any, near_ref, w_ref, *refs):
    tb_ref, x_ref, xc_ref, y_ref, yc_ref, xs_ref, ys_ref, gx_ref, gy_ref, sum_ref = refs[:10]
    sem = refs[10]
    copies = [
        pltpu.make_async_copy(x_any, x_ref, sem.at[0]),
        pltpu.make_async_copy(y_any, y_ref, sem.at[1]),
    ]
    for copy in copies:
        copy.start()
    count = near_ref.shape[0]
    near = near_ref[...] * scale_of(near_ref[...])
    for copy, ref, scale_ref in zip(copies, (x_ref, y_ref), (xc_ref, yc_ref)):
        copy.wait()
        scale_ref[...] = scale_of(ref[...])
        ref[...] = ref[...] * scale_ref[...]
    xs_ref[...] = stacked(x_ref[...])
    ys_ref[...] = stacked(jnp.concatenate([y_ref[...], near], axis=0))
    tb_ref[0:1, :] = jnp.exp(jnp.full((1, count), lt[0], F32))
    tb_ref[1:2, :] = jnp.full((1, count), bi[0], F32)
    temper, bias = scalars_of(tb_ref)
    rows = lax.broadcasted_iota(jnp.int32, (2 * count, count), 0)
    cols = lax.broadcasted_iota(jnp.int32, (2 * count, count), 1)
    z = temper * mm(ys_ref, xs_ref, NT) + bias
    loss, slope = gated(z, w_ref[...] * temper, rows == cols)
    sum_ref[...] = jnp.sum(loss, axis=0, keepdims=True)
    gx_ref[...] = mm(stacked(slope.T), ys_ref, NN)
    gy_ref[...] = mm(stacked(slope), xs_ref, NN)


def second_body(others, tb_ref, *refs):
    raw_refs, refs = refs[:others], refs[others:]
    w_refs, refs = refs[:others], refs[others:]
    xs_ref, ys_ref, all_ref, refs = *refs[:3], refs[3:]
    gp_refs, refs = refs[:others], refs[others:]
    sump_refs, slope_refs = refs[:others], refs[others:]
    temper, bias = scalars_of(tb_ref)
    count = raw_refs[0].shape[0]
    deep = (others + 1) * count
    eye = square(count)
    all_ref[:count] = xs_ref[:count]
    all_ref[deep : deep + count] = xs_ref[count:]
    for s in range(others):
        raw = raw_refs[s][...]
        px = stacked(raw * scale_of(raw))
        here = (s + 1) * count
        all_ref[here : here + count] = px[:count]
        all_ref[deep + here : deep + here + count] = px[count:]
        z = temper * mm(px, ys_ref, NT) + bias
        weight = jnp.sum(jnp.where(eye, w_refs[s][...], 0.0), axis=1, keepdims=True)
        loss, slope = gated(z, weight * temper)
        sums = jnp.sum(loss, axis=1, keepdims=True)
        sump_refs[s][...] = jnp.sum(jnp.where(eye, sums, 0.0), axis=0, keepdims=True)
        slope_refs[s][...] = slope
        gp_refs[s][...] = mm(stacked(slope), ys_ref, NN)


def third_body(others, tb_ref, *refs):
    members = others + 1
    far_ref, refs = refs[0], refs[1:]
    w_refs, refs = refs[:members], refs[members:]
    all_ref, refs = refs[0], refs[1:]
    gp_in, refs = refs[:others], refs[others:]
    sum_in, refs = refs[:members], refs[members:]
    gfar_ref, refs = refs[0], refs[1:]
    gp_refs, refs = refs[:others], refs[others:]
    sum_refs, refs = refs[:members], refs[members:]
    fs_ref, slope_ref = refs
    temper, bias = scalars_of(tb_ref)
    count = far_ref.shape[0]
    far = far_ref[...]
    fs_ref[...] = stacked(far)
    scale = scale_of(far)
    z = (temper * scale) * mm(fs_ref, all_ref, NT) + bias
    weight = jnp.concatenate([w[...] for w in w_refs], axis=1) * temper
    loss, slope = gated(z, weight)
    gfar_ref[...] = mm(stacked(slope), all_ref, NN)
    slope = slope * scale
    sums = jnp.sum(loss, axis=0, keepdims=True)
    for s in range(members):
        part = slice(s * count, (s + 1) * count)
        sum_refs[s][...] = sum_in[s][...] + sums[:, part]
        if s == 0:
            slope_ref[...] = slope[:, part]
        else:
            gp_refs[s - 1][...] = gp_in[s - 1][...] + mm(stacked(slope[:, part].T), fs_ref, NN)


def fourth_body(others, gx_in, gy_in, slope_ref, fs_ref, all_ref, *refs):
    slopes, (gx_ref, gown_ref, gnear_ref) = refs[:others], refs[others:]
    count = gx_in.shape[0]
    deep = (others + 1) * count
    gy = gy_in[...]
    for s in range(others):
        here = (s + 1) * count
        px = jnp.concatenate(
            [all_ref[here : here + count], all_ref[deep + here : deep + here + count]], axis=0
        )
        gy = gy + mm(stacked(slopes[s][...].T), px, NN)
    gown_ref[...] = gy[:count]
    gnear_ref[...] = gy[count:]
    gx_ref[...] = gx_in[...] + mm(stacked(slope_ref[...].T), fs_ref, NN)


def last_body(others, pairs, *refs):
    (unit_x, scale_x, own_x), refs = refs[:3], refs[3:]
    back_x, refs = refs[:others], refs[others:]
    (unit_y, scale_y, own_y, near_y, far_y), refs = refs[:5], refs[5:]
    sums, refs = refs[: others + 1], refs[others + 1 :]
    x_out, y_out, loss_out, held, line, sem = refs
    rows = unit_x.shape[0] // CHUNKS
    copies = []

    def send(source, target):
        copies.append(pltpu.make_async_copy(source, target, sem.at[len(copies)]))
        copies[-1].start()

    def through(k, here, unit, scale, grad, out_ref):
        inner = jnp.sum(unit * grad, axis=1, keepdims=True)
        held[k, here, :] = scale * (grad - unit * inner)
        send(held.at[k, here, :], out_ref.at[here, :])

    total = sums[0][...]
    for r in sums[1:]:
        total = total + r[...]
    line[...] = total / pairs
    send(line, loss_out)
    for c in range(CHUNKS):
        here = pl.ds(c * rows, rows)
        grad = own_x[here, :]
        for r in back_x:
            grad = grad + r[here, :]
        through(0, here, unit_x[here, :], scale_x[here, :], grad, x_out)
    for c in range(CHUNKS):
        here = pl.ds(c * rows, rows)
        grad = own_y[here, :] + near_y[here, :] + far_y[here, :]
        through(1, here, unit_y[here, :], scale_y[here, :], grad, y_out)
    for copy in copies:
        copy.wait()


def shape(*dims, kind=F32):
    return jax.ShapeDtypeStruct(dims, kind)


PARAMS = pltpu.CompilerParams(vmem_limit_bytes=16 * 1024 * 1024)


def in_hbm(args):
    return [pltpu.with_memory_space_constraint(a, pltpu.HBM) for a in args]


def in_vmem(args):
    return [pltpu.with_memory_space_constraint(a, pltpu.VMEM) for a in args]


def call(body, outs, *args, scratch=(), scalars=0, anywhere=0):
    numbers, args = args[:scalars], args[scalars:]
    return pl.pallas_call(
        body,
        out_shape=[pltpu.VMEM(o.shape, o.dtype) for o in outs],
        in_specs=[SMEM] * scalars + [HBM] * anywhere + [VMEM] * (len(args) - anywhere),
        out_specs=[VMEM] * len(outs),
        scratch_shapes=list(scratch),
        compiler_params=PARAMS,
    )(*numbers, *in_hbm(args[:anywhere]), *in_vmem(args[anywhere:]))


def finish(others, pairs, *args):
    full = shape(*args[0].shape)
    line = shape(1, full.shape[0])
    return pl.pallas_call(
        functools.partial(last_body, others, pairs),
        out_shape=[full, full, line],
        in_specs=[VMEM] * len(args),
        out_specs=[HBM] * 3,
        scratch_shapes=[
            pltpu.VMEM((2, *full.shape), F32),
            pltpu.VMEM(line.shape, F32),
            pltpu.SemaphoreType.DMA((2 * CHUNKS + 1,)),
        ],
        compiler_params=PARAMS,
    )(*in_vmem(args))


def body(images, texts, log_temp, bias, row_weight):
    members = lax.axis_size("grp")
    others = members - 1
    count, width = images.shape
    weight = row_weight.reshape(1, count)
    length = lax.axis_size("blk")
    near_pairs = [(i, i + 1) for i in range(0, length, 2)]
    far_pairs = [(i, (i + 1) % length) for i in range(1, length, 2)]
    raws = [shifted(images, "grp", -s) for s in range(1, members)]
    far = exchanged(texts, "blk", far_pairs)
    near = exchanged(texts, "blk", near_pairs)
    weights = [weight] + [shifted(weight, "grp", -s) for s in range(1, members)]
    full = shape(count, width)
    line = shape(1, count)
    stack = shape(2 * count, width, kind=BF)
    tb, unit_x, scale_x, unit_y, scale_y, xs, ys, gx, gy, sums = call(
        first_body,
        [
            shape(2, count),
            full,
            shape(count, 1),
            full,
            shape(count, 1),
            stack,
            shape(4 * count, width, kind=BF),
            full,
            shape(2 * count, width),
            line,
        ],
        log_temp,
        bias,
        images,
        texts,
        near,
        weight,
        scratch=[pltpu.SemaphoreType.DMA((2,))],
        scalars=2,
        anywhere=2,
    )
    outs = call(
        functools.partial(second_body, others),
        [shape(2 * members * count, width, kind=BF)]
        + [full] * others
        + [line] * others
        + [shape(count, 2 * count)] * others,
        tb,
        *raws,
        *weights[1:],
        xs,
        ys,
    )
    everyone, outs = outs[0], outs[1:]
    gp, outs = outs[:others], outs[others:]
    sump, slopes = outs[:others], outs[others:]
    outs = call(
        functools.partial(third_body, others),
        [full] + [full] * others + [line] * members + [stack, shape(count, count)],
        tb,
        far,
        *weights,
        everyone,
        *gp,
        sums,
        *sump,
    )
    g_far, outs = outs[0], outs[1:]
    gp, outs = outs[:others], outs[others:]
    sums, (fs, slope) = outs[:members], outs[members:]
    back_x = [shifted(gp[s - 1], "grp", s) for s in range(1, members)]
    back_far = exchanged(g_far, "blk", far_pairs)
    back_sum = [shifted(sums[s], "grp", s) for s in range(1, members)]
    gx, g_own, g_near = call(
        functools.partial(fourth_body, others),
        [full] * 3,
        gx,
        gy,
        slope,
        fs,
        everyone,
        *slopes,
    )
    back_near = exchanged(g_near, "blk", near_pairs)
    grad_x, grad_y, row_loss = finish(
        others,
        3.0 * members * count,
        unit_x,
        scale_x,
        gx,
        *back_x,
        unit_y,
        scale_y,
        g_own,
        back_near,
        back_far,
        sums[0],
        *back_sum,
    )
    return (row_loss.reshape(count), grad_x, grad_y)


def solution(mesh):
    placed = (P(("blk", "grp"), None), P(("blk", "grp"), None), P(), P(), P(("blk", "grp")))
    return jax.shard_map(
        body,
        mesh=mesh,
        in_specs=placed,
        out_specs=(P(("blk", "grp")), P(("blk", "grp"), None), P(("blk", "grp"), None)),
        check_vma=False,
    )
```

```python
import functools

import jax
import jax.numpy as jnp
from jax import lax
from jax.experimental import pallas as pl
from jax.experimental.pallas import tpu as pltpu
from jax.sharding import PartitionSpec as P


BF = jnp.bfloat16
F32 = jnp.float32
VMEM = pl.BlockSpec(memory_space=pltpu.VMEM)
SMEM = pl.BlockSpec(memory_space=pltpu.SMEM)
HBM = pl.BlockSpec(memory_space=pltpu.HBM)
CHUNKS = 4
NT = ((1,), (1,))
NN = ((1,), (0,))


def exchanged(x, axis, pairs):
    return lax.ppermute(x, axis, pairs + [(b, a) for (a, b) in pairs])


def shifted(x, axis, by):
    length = lax.axis_size(axis)
    return lax.ppermute(x, axis, [(i, (i + by) % length) for i in range(length)])


def stacked(v):
    high = v.astype(BF)
    return jnp.concatenate([high, (v - high.astype(F32)).astype(BF)], axis=0)


def mm(a, b, dims):
    rows = a.shape[0] // 2
    deep = b.shape[0] // 2

    def one(p, q):
        return lax.dot_general(p, q, (dims, ((), ())), preferred_element_type=F32)

    both = one(a[...], b[:deep])
    return both[:rows] + (both[rows:] + one(a[:rows], b[deep:]))


def log_one_plus(t):
    series = t * (1.0 + t * (-0.5 + t * (1.0 / 3.0 + t * (-0.25 + t * 0.2))))
    return jnp.where(t < 0.03125, series, jnp.log(1.0 + t))


def gated(z, weight, diagonal=None):
    signed = z if diagonal is None else jnp.where(diagonal, -z, z)
    small = jnp.exp(-jnp.abs(signed))
    loss = jnp.maximum(signed, 0.0) + log_one_plus(small)
    slope = jnp.where(signed >= 0.0, 1.0, small) / (1.0 + small) * weight
    if diagonal is not None:
        slope = jnp.where(diagonal, -slope, slope)
    return loss, slope


def scale_of(raw):
    return lax.rsqrt(jnp.sum(raw * raw, axis=1, keepdims=True) + 1e-06)


def square(count):
    rows = lax.broadcasted_iota(jnp.int32, (count, count), 0)
    return rows == lax.broadcasted_iota(jnp.int32, (count, count), 1)


def scalars_of(tb_ref):
    return tb_ref[0:1, 0:1], tb_ref[1:2, 0:1]


def first_body(lt, bi, x_any, y_any, near_ref, w_ref, *refs):
    tb_ref, x_ref, xc_ref, y_ref, yc_ref, xs_ref, ys_ref, gx_ref, gy_ref, sum_ref = refs[:10]
    sem = refs[10]
    copies = [
        pltpu.make_async_copy(x_any, x_ref, sem.at[0]),
        pltpu.make_async_copy(y_any, y_ref, sem.at[1]),
    ]
    for copy in copies:
        copy.start()
    count = near_ref.shape[0]
    near = near_ref[...] * scale_of(near_ref[...])
    for copy, ref, scale_ref in zip(copies, (x_ref, y_ref), (xc_ref, yc_ref)):
        copy.wait()
        scale_ref[...] = scale_of(ref[...])
        ref[...] = ref[...] * scale_ref[...]
    xs_ref[...] = stacked(x_ref[...])
    ys_ref[...] = stacked(jnp.concatenate([y_ref[...], near], axis=0))
    tb_ref[0:1, :] = jnp.exp(jnp.full((1, count), lt[0], F32))
    tb_ref[1:2, :] = jnp.full((1, count), bi[0], F32)
    temper, bias = scalars_of(tb_ref)
    rows = lax.broadcasted_iota(jnp.int32, (2 * count, count), 0)
    cols = lax.broadcasted_iota(jnp.int32, (2 * count, count), 1)
    z = temper * mm(ys_ref, xs_ref, NT) + bias
    loss, slope = gated(z, w_ref[...] * temper, rows == cols)
    sum_ref[...] = jnp.sum(loss, axis=0, keepdims=True)
    gx_ref[...] = mm(stacked(slope.T), ys_ref, NN)
    gy_ref[...] = mm(stacked(slope), xs_ref, NN)


def second_body(others, tb_ref, *refs):
    raw_refs, refs = refs[:others], refs[others:]
    w_refs, refs = refs[:others], refs[others:]
    xs_ref, ys_ref, gy_in, all_ref, gnear_ref, refs = *refs[:5], refs[5:]
    gp_refs, refs = refs[:others], refs[others:]
    sump_refs, slope_refs = refs[:others], refs[others:]
    temper, bias = scalars_of(tb_ref)
    count = raw_refs[0].shape[0]
    deep = (others + 1) * count
    eye = square(count)
    all_ref[:count] = xs_ref[:count]
    all_ref[deep : deep + count] = xs_ref[count:]
    near = gy_in[count:]
    for s in range(others):
        raw = raw_refs[s][...]
        px = stacked(raw * scale_of(raw))
        here = (s + 1) * count
        all_ref[here : here + count] = px[:count]
        all_ref[deep + here : deep + here + count] = px[count:]
        z = temper * mm(px, ys_ref, NT) + bias
        weight = jnp.sum(jnp.where(eye, w_refs[s][...], 0.0), axis=1, keepdims=True)
        loss, slope = gated(z, weight * temper)
        sums = jnp.sum(loss, axis=1, keepdims=True)
        sump_refs[s][...] = jnp.sum(jnp.where(eye, sums, 0.0), axis=0, keepdims=True)
        slope_refs[s][...] = slope[:, :count]
        near = near + mm(stacked(slope[:, count:].T), px, NN)
        gp_refs[s][...] = mm(stacked(slope), ys_ref, NN)
    gnear_ref[...] = near


def third_body(others, tb_ref, *refs):
    members = others + 1
    far_ref, refs = refs[0], refs[1:]
    w_refs, refs = refs[:members], refs[members:]
    all_ref, refs = refs[0], refs[1:]
    gp_in, refs = refs[:others], refs[others:]
    sum_in, refs = refs[:members], refs[members:]
    gfar_ref, refs = refs[0], refs[1:]
    gp_refs, refs = refs[:others], refs[others:]
    sum_refs, refs = refs[:members], refs[members:]
    fs_ref, slope_ref = refs
    temper, bias = scalars_of(tb_ref)
    count = far_ref.shape[0]
    far = far_ref[...]
    fs_ref[...] = stacked(far)
    scale = scale_of(far)
    z = (temper * scale) * mm(fs_ref, all_ref, NT) + bias
    weight = jnp.concatenate([w[...] for w in w_refs], axis=1) * temper
    loss, slope = gated(z, weight)
    gfar_ref[...] = mm(stacked(slope), all_ref, NN)
    slope = slope * scale
    sums = jnp.sum(loss, axis=0, keepdims=True)
    for s in range(members):
        part = slice(s * count, (s + 1) * count)
        sum_refs[s][...] = sum_in[s][...] + sums[:, part]
        if s == 0:
            slope_ref[...] = slope[:, part]
        else:
            gp_refs[s - 1][...] = gp_in[s - 1][...] + mm(stacked(slope[:, part].T), fs_ref, NN)


def fourth_body(others, gx_in, gy_in, slope_ref, fs_ref, all_ref, *refs):
    slopes, (gx_ref, gown_ref) = refs[:others], refs[others:]
    count = gx_in.shape[0]
    deep = (others + 1) * count
    gy = gy_in[:count]
    for s in range(others):
        here = (s + 1) * count
        px = jnp.concatenate(
            [all_ref[here : here + count], all_ref[deep + here : deep + here + count]], axis=0
        )
        gy = gy + mm(stacked(slopes[s][...].T), px, NN)
    gown_ref[...] = gy
    gx_ref[...] = gx_in[...] + mm(stacked(slope_ref[...].T), fs_ref, NN)


def last_body(others, pairs, *refs):
    (unit_x, scale_x, own_x), refs = refs[:3], refs[3:]
    back_x, refs = refs[:others], refs[others:]
    (unit_y, scale_y, own_y, near_y, far_y), refs = refs[:5], refs[5:]
    sums, refs = refs[: others + 1], refs[others + 1 :]
    x_out, y_out, loss_out, held, line, sem = refs
    rows = unit_x.shape[0] // CHUNKS
    copies = []

    def send(source, target):
        copies.append(pltpu.make_async_copy(source, target, sem.at[len(copies)]))
        copies[-1].start()

    total = sums[0][...]
    for r in sums[1:]:
        total = total + r[...]
    line[...] = total / pairs
    send(line, loss_out)
    sides = [
        (unit_x, scale_x, [own_x, *back_x], x_out),
        (unit_y, scale_y, [own_y, near_y, far_y], y_out),
    ]
    inners = []
    for k, (unit, _, grads, _) in enumerate(sides):
        grad = grads[0][...]
        for r in grads[1:]:
            grad = grad + r[...]
        held[k] = grad
        inners.append(jnp.sum(unit[...] * grad, axis=1, keepdims=True))
    for k, (unit, scale, _, out_ref) in enumerate(sides):
        for c in range(CHUNKS):
            low, high = c * rows, (c + 1) * rows
            inner = inners[k][low:high]
            held[k, low:high] = scale[low:high] * (held[k, low:high] - unit[low:high] * inner)
            send(held.at[k, pl.ds(low, rows), :], out_ref.at[pl.ds(low, rows), :])
    for copy in copies:
        copy.wait()


def shape(*dims, kind=F32):
    return jax.ShapeDtypeStruct(dims, kind)


PARAMS = pltpu.CompilerParams(vmem_limit_bytes=16 * 1024 * 1024)


def in_hbm(args):
    return [pltpu.with_memory_space_constraint(a, pltpu.HBM) for a in args]


def in_vmem(args):
    return [pltpu.with_memory_space_constraint(a, pltpu.VMEM) for a in args]


def call(body, outs, *args, scratch=(), scalars=0, anywhere=0):
    numbers, args = args[:scalars], args[scalars:]
    return pl.pallas_call(
        body,
        out_shape=[pltpu.VMEM(o.shape, o.dtype) for o in outs],
        in_specs=[SMEM] * scalars + [HBM] * anywhere + [VMEM] * (len(args) - anywhere),
        out_specs=[VMEM] * len(outs),
        scratch_shapes=list(scratch),
        compiler_params=PARAMS,
    )(*numbers, *in_hbm(args[:anywhere]), *in_vmem(args[anywhere:]))


def finish(others, pairs, *args):
    full = shape(*args[0].shape)
    line = shape(1, full.shape[0])
    return pl.pallas_call(
        functools.partial(last_body, others, pairs),
        out_shape=[full, full, line],
        in_specs=[VMEM] * len(args),
        out_specs=[HBM] * 3,
        scratch_shapes=[
            pltpu.VMEM((2, *full.shape), F32),
            pltpu.VMEM(line.shape, F32),
            pltpu.SemaphoreType.DMA((2 * CHUNKS + 1,)),
        ],
        compiler_params=PARAMS,
    )(*in_vmem(args))


def body(images, texts, log_temp, bias, row_weight):
    members = lax.axis_size("grp")
    others = members - 1
    count, width = images.shape
    weight = row_weight.reshape(1, count)
    length = lax.axis_size("blk")
    near_pairs = [(i, i + 1) for i in range(0, length, 2)]
    far_pairs = [(i, (i + 1) % length) for i in range(1, length, 2)]
    raws = [shifted(images, "grp", -s) for s in range(1, members)]
    far = exchanged(texts, "blk", far_pairs)
    near = exchanged(texts, "blk", near_pairs)
    weights = [weight] + [shifted(weight, "grp", -s) for s in range(1, members)]
    full = shape(count, width)
    line = shape(1, count)
    stack = shape(2 * count, width, kind=BF)
    tb, unit_x, scale_x, unit_y, scale_y, xs, ys, gx, gy, sums = call(
        first_body,
        [
            shape(2, count),
            full,
            shape(count, 1),
            full,
            shape(count, 1),
            stack,
            shape(4 * count, width, kind=BF),
            full,
            shape(2 * count, width),
            line,
        ],
        log_temp,
        bias,
        images,
        texts,
        near,
        weight,
        scratch=[pltpu.SemaphoreType.DMA((2,))],
        scalars=2,
        anywhere=2,
    )
    outs = call(
        functools.partial(second_body, others),
        [shape(2 * members * count, width, kind=BF), full]
        + [full] * others
        + [line] * others
        + [shape(count, count)] * others,
        tb,
        *raws,
        *weights[1:],
        xs,
        ys,
        gy,
    )
    everyone, g_near, outs = outs[0], outs[1], outs[2:]
    gp, outs = outs[:others], outs[others:]
    sump, slopes = outs[:others], outs[others:]
    back_near = exchanged(g_near, "blk", near_pairs)
    outs = call(
        functools.partial(third_body, others),
        [full] + [full] * others + [line] * members + [stack, shape(count, count)],
        tb,
        far,
        *weights,
        everyone,
        *gp,
        sums,
        *sump,
    )
    g_far, outs = outs[0], outs[1:]
    gp, outs = outs[:others], outs[others:]
    sums, (fs, slope) = outs[:members], outs[members:]
    back_x = [shifted(gp[s - 1], "grp", s) for s in range(1, members)]
    back_far = exchanged(g_far, "blk", far_pairs)
    back_sum = [shifted(sums[s], "grp", s) for s in range(1, members)]
    gx, g_own = call(
        functools.partial(fourth_body, others),
        [full] * 2,
        gx,
        gy,
        slope,
        fs,
        everyone,
        *slopes,
    )
    grad_x, grad_y, row_loss = finish(
        others,
        3.0 * members * count,
        unit_x,
        scale_x,
        gx,
        *back_x,
        unit_y,
        scale_y,
        g_own,
        back_near,
        back_far,
        sums[0],
        *back_sum,
    )
    return (row_loss.reshape(count), grad_x, grad_y)


def solution(mesh):
    placed = (P(("blk", "grp"), None), P(("blk", "grp"), None), P(), P(), P(("blk", "grp")))
    return jax.shard_map(
        body,
        mesh=mesh,
        in_specs=placed,
        out_specs=(P(("blk", "grp")), P(("blk", "grp"), None), P(("blk", "grp"), None)),
        check_vma=False,
    )
```

```python
import functools

import jax
import jax.numpy as jnp
from jax import lax
from jax.experimental import pallas as pl
from jax.experimental.pallas import tpu as pltpu
from jax.sharding import PartitionSpec as P


BF = jnp.bfloat16
F32 = jnp.float32
VMEM = pl.BlockSpec(memory_space=pltpu.VMEM)
SMEM = pl.BlockSpec(memory_space=pltpu.SMEM)
HBM = pl.BlockSpec(memory_space=pltpu.HBM)
CHUNKS = 4
NT = ((1,), (1,))
NN = ((1,), (0,))


def exchanged(x, axis, pairs):
    return lax.ppermute(x, axis, pairs + [(b, a) for (a, b) in pairs])


def mixed_pairs(length, members):
    first, second = [], []
    for b in range(length):
        far = (b + 1) % length if b % 2 else (b - 1) % length
        for g in range(members):
            here = b * members + g
            across = (here, far * members + g)
            along = (here, b * members + (g + 1) % members)
            direct = length % 4 == 0 and b % 4 in (1, 2)
            first.append(across if direct else along)
            second.append(along if direct else across)
    return first, second


def far_goes_first():
    place = lax.axis_index("blk")
    return (lax.axis_size("blk") % 4 == 0) & (lax.rem(place + 1, 4) >= 2)


def shifted(x, axis, by):
    length = lax.axis_size(axis)
    return lax.ppermute(x, axis, [(i, (i + by) % length) for i in range(length)])


def stacked(v):
    high = v.astype(BF)
    return jnp.concatenate([high, (v - high.astype(F32)).astype(BF)], axis=0)


def mm(a, b, dims):
    rows = a.shape[0] // 2
    deep = b.shape[0] // 2

    def one(p, q):
        return lax.dot_general(p, q, (dims, ((), ())), preferred_element_type=F32)

    both = one(a[...], b[:deep])
    return both[:rows] + (both[rows:] + one(a[:rows], b[deep:]))


def log_one_plus(t):
    series = t * (1.0 + t * (-0.5 + t * (1.0 / 3.0 + t * (-0.25 + t * 0.2))))
    return jnp.where(t < 0.03125, series, jnp.log(1.0 + t))


def gated(z, weight, diagonal=None):
    signed = z if diagonal is None else jnp.where(diagonal, -z, z)
    small = jnp.exp(-jnp.abs(signed))
    loss = jnp.maximum(signed, 0.0) + log_one_plus(small)
    slope = jnp.where(signed >= 0.0, 1.0, small) / (1.0 + small) * weight
    if diagonal is not None:
        slope = jnp.where(diagonal, -slope, slope)
    return loss, slope


def scale_of(raw):
    return lax.rsqrt(jnp.sum(raw * raw, axis=1, keepdims=True) + 1e-06)


def square(count):
    rows = lax.broadcasted_iota(jnp.int32, (count, count), 0)
    return rows == lax.broadcasted_iota(jnp.int32, (count, count), 1)


def scalars_of(tb_ref):
    return tb_ref[0:1, 0:1], tb_ref[1:2, 0:1]


def first_body(lt, bi, x_any, y_any, near_ref, w_ref, *refs):
    tb_ref, x_ref, xc_ref, y_ref, yc_ref, xs_ref, ys_ref, gx_ref, gy_ref, sum_ref = refs[:10]
    sem = refs[10]
    copies = [
        pltpu.make_async_copy(x_any, x_ref, sem.at[0]),
        pltpu.make_async_copy(y_any, y_ref, sem.at[1]),
    ]
    for copy in copies:
        copy.start()
    count = near_ref.shape[0]
    near = near_ref[...] * scale_of(near_ref[...])
    for copy, ref, scale_ref in zip(copies, (x_ref, y_ref), (xc_ref, yc_ref)):
        copy.wait()
        scale_ref[...] = scale_of(ref[...])
        ref[...] = ref[...] * scale_ref[...]
    xs_ref[...] = stacked(x_ref[...])
    ys_ref[...] = stacked(jnp.concatenate([y_ref[...], near], axis=0))
    tb_ref[0:1, :] = jnp.exp(jnp.full((1, count), lt[0], F32))
    tb_ref[1:2, :] = jnp.full((1, count), bi[0], F32)
    temper, bias = scalars_of(tb_ref)
    rows = lax.broadcasted_iota(jnp.int32, (2 * count, count), 0)
    cols = lax.broadcasted_iota(jnp.int32, (2 * count, count), 1)
    z = temper * mm(ys_ref, xs_ref, NT) + bias
    loss, slope = gated(z, w_ref[...] * temper, rows == cols)
    sum_ref[...] = jnp.sum(loss, axis=0, keepdims=True)
    gx_ref[...] = mm(stacked(slope.T), ys_ref, NN)
    gy_ref[...] = mm(stacked(slope), xs_ref, NN)


def second_body(others, tb_ref, *refs):
    raw_refs, refs = refs[:others], refs[others:]
    w_refs, refs = refs[:others], refs[others:]
    xs_ref, ys_ref, all_ref, refs = *refs[:3], refs[3:]
    gp_refs, refs = refs[:others], refs[others:]
    sump_refs, slope_refs = refs[:others], refs[others:]
    temper, bias = scalars_of(tb_ref)
    count = raw_refs[0].shape[0]
    deep = (others + 1) * count
    eye = square(count)
    all_ref[:count] = xs_ref[:count]
    all_ref[deep : deep + count] = xs_ref[count:]
    for s in range(others):
        raw = raw_refs[s][...]
        px = stacked(raw * scale_of(raw))
        here = (s + 1) * count
        all_ref[here : here + count] = px[:count]
        all_ref[deep + here : deep + here + count] = px[count:]
        z = temper * mm(px, ys_ref, NT) + bias
        weight = jnp.sum(jnp.where(eye, w_refs[s][...], 0.0), axis=1, keepdims=True)
        loss, slope = gated(z, weight * temper)
        sums = jnp.sum(loss, axis=1, keepdims=True)
        sump_refs[s][...] = jnp.sum(jnp.where(eye, sums, 0.0), axis=0, keepdims=True)
        slope_refs[s][...] = slope
        gp_refs[s][...] = mm(stacked(slope), ys_ref, NN)


def third_body(others, tb_ref, *refs):
    members = others + 1
    far_ref, refs = refs[0], refs[1:]
    w_refs, refs = refs[:members], refs[members:]
    all_ref, refs = refs[0], refs[1:]
    gp_in, refs = refs[:others], refs[others:]
    sum_in, refs = refs[:members], refs[members:]
    one_ref, two_ref, refs = *refs[:2], refs[2:]
    gp_refs, refs = refs[: others - 1], refs[others - 1 :]
    sum_refs, refs = refs[:members], refs[members:]
    fs_ref, slope_ref, both_ref, turned_ref = refs
    temper, bias = scalars_of(tb_ref)
    count = far_ref.shape[0]
    far = far_ref[...]
    fs_ref[...] = stacked(far)
    scale = scale_of(far)
    z = (temper * scale) * mm(fs_ref, all_ref, NT) + bias
    weight = jnp.concatenate([w[...] for w in w_refs], axis=1) * temper
    loss, slope = gated(z, weight)
    both_ref[...] = stacked(slope)
    slope = slope * scale
    sums = jnp.sum(loss, axis=0, keepdims=True)
    for s in range(members):
        part = slice(s * count, (s + 1) * count)
        sum_refs[s][...] = sum_in[s][...] + sums[:, part]
        if s == 0:
            slope_ref[...] = slope[:, part]
        else:
            turned_ref[s - 1] = stacked(slope[:, part].T)
            if s > 1:
                gp_refs[s - 2][...] = gp_in[s - 1][...] + mm(turned_ref[s - 1], fs_ref, NN)

    def finish_into(far_out, next_out):
        far_out[...] = mm(both_ref, all_ref, NN)
        next_out[...] = gp_in[0][...] + mm(turned_ref[0], fs_ref, NN)

    far_first = far_goes_first()
    pl.when(far_first)(lambda: finish_into(one_ref, two_ref))
    pl.when(jnp.logical_not(far_first))(lambda: finish_into(two_ref, one_ref))


def fourth_body(others, gx_in, gy_in, slope_ref, fs_ref, all_ref, *refs):
    slopes, (gx_ref, gown_ref, gnear_ref) = refs[:others], refs[others:]
    count = gx_in.shape[0]
    deep = (others + 1) * count
    gy = gy_in[...]
    for s in range(others):
        here = (s + 1) * count
        px = jnp.concatenate(
            [all_ref[here : here + count], all_ref[deep + here : deep + here + count]], axis=0
        )
        gy = gy + mm(stacked(slopes[s][...].T), px, NN)
    gown_ref[...] = gy[:count]
    gnear_ref[...] = gy[count:]
    gx_ref[...] = gx_in[...] + mm(stacked(slope_ref[...].T), fs_ref, NN)


def last_body(others, pairs, *refs):
    (unit_x, scale_x, own_x), refs = refs[:3], refs[3:]
    back_x, refs = refs[: others - 1], refs[others - 1 :]
    (unit_y, scale_y, own_y, near_y, one, two), refs = refs[:6], refs[6:]
    sums, refs = refs[: others + 1], refs[others + 1 :]
    x_out, y_out, loss_out, held, line, sem = refs
    rows = unit_x.shape[0] // CHUNKS
    total = sums[0][...]
    for r in sums[1:]:
        total = total + r[...]
    line[...] = total / pairs

    def run(far_y, next_x):
        copies = []

        def send(source, target):
            copies.append(pltpu.make_async_copy(source, target, sem.at[len(copies)]))
            copies[-1].start()

        send(line, loss_out)
        sides = [
            (unit_x, scale_x, [own_x, next_x, *back_x], x_out),
            (unit_y, scale_y, [own_y, near_y, far_y], y_out),
        ]
        for k, (unit_ref, scale_ref, grads, out_ref) in enumerate(sides):
            for c in range(CHUNKS):
                here = pl.ds(c * rows, rows)
                grad = grads[0][here, :]
                for r in grads[1:]:
                    grad = grad + r[here, :]
                unit = unit_ref[here, :]
                inner = jnp.sum(unit * grad, axis=1, keepdims=True)
                held[k, here, :] = scale_ref[here, :] * (grad - unit * inner)
                send(held.at[k, here, :], out_ref.at[here, :])
        for copy in copies:
            copy.wait()

    far_first = far_goes_first()
    pl.when(far_first)(lambda: run(one, two))
    pl.when(jnp.logical_not(far_first))(lambda: run(two, one))


def shape(*dims, kind=F32):
    return jax.ShapeDtypeStruct(dims, kind)


PARAMS = pltpu.CompilerParams(vmem_limit_bytes=16 * 1024 * 1024)


def in_hbm(args):
    return [pltpu.with_memory_space_constraint(a, pltpu.HBM) for a in args]


def in_vmem(args):
    return [pltpu.with_memory_space_constraint(a, pltpu.VMEM) for a in args]


def call(body, outs, *args, scratch=(), scalars=0, anywhere=0):
    numbers, args = args[:scalars], args[scalars:]
    return pl.pallas_call(
        body,
        out_shape=[pltpu.VMEM(o.shape, o.dtype) for o in outs],
        in_specs=[SMEM] * scalars + [HBM] * anywhere + [VMEM] * (len(args) - anywhere),
        out_specs=[VMEM] * len(outs),
        scratch_shapes=list(scratch),
        compiler_params=PARAMS,
    )(*numbers, *in_hbm(args[:anywhere]), *in_vmem(args[anywhere:]))


def finish(others, pairs, *args):
    full = shape(*args[0].shape)
    line = shape(1, full.shape[0])
    return pl.pallas_call(
        functools.partial(last_body, others, pairs),
        out_shape=[full, full, line],
        in_specs=[VMEM] * len(args),
        out_specs=[HBM] * 3,
        scratch_shapes=[
            pltpu.VMEM((2, *full.shape), F32),
            pltpu.VMEM(line.shape, F32),
            pltpu.SemaphoreType.DMA((2 * CHUNKS + 1,)),
        ],
        compiler_params=PARAMS,
    )(*in_vmem(args))


def body(images, texts, log_temp, bias, row_weight):
    members = lax.axis_size("grp")
    others = members - 1
    count, width = images.shape
    weight = row_weight.reshape(1, count)
    length = lax.axis_size("blk")
    near_pairs = [(i, i + 1) for i in range(0, length, 2)]
    far_pairs = [(i, (i + 1) % length) for i in range(1, length, 2)]
    raws = [shifted(images, "grp", -s) for s in range(1, members)]
    far = exchanged(texts, "blk", far_pairs)
    near = exchanged(texts, "blk", near_pairs)
    weights = [weight] + [shifted(weight, "grp", -s) for s in range(1, members)]
    full = shape(count, width)
    line = shape(1, count)
    stack = shape(2 * count, width, kind=BF)
    tb, unit_x, scale_x, unit_y, scale_y, xs, ys, gx, gy, sums = call(
        first_body,
        [
            shape(2, count),
            full,
            shape(count, 1),
            full,
            shape(count, 1),
            stack,
            shape(4 * count, width, kind=BF),
            full,
            shape(2 * count, width),
            line,
        ],
        log_temp,
        bias,
        images,
        texts,
        near,
        weight,
        scratch=[pltpu.SemaphoreType.DMA((2,))],
        scalars=2,
        anywhere=2,
    )
    outs = call(
        functools.partial(second_body, others),
        [shape(2 * members * count, width, kind=BF)]
        + [full] * others
        + [line] * others
        + [shape(count, 2 * count)] * others,
        tb,
        *raws,
        *weights[1:],
        xs,
        ys,
    )
    everyone, outs = outs[0], outs[1:]
    gp, outs = outs[:others], outs[others:]
    sump, slopes = outs[:others], outs[others:]
    outs = call(
        functools.partial(third_body, others),
        [full, full]
        + [full] * (others - 1)
        + [line] * members
        + [stack, shape(count, count)],
        tb,
        far,
        *weights,
        everyone,
        *gp,
        sums,
        *sump,
        scratch=[
            pltpu.VMEM((2 * count, members * count), BF),
            pltpu.VMEM((others, 2 * count, count), BF),
        ],
    )
    one, two, outs = outs[0], outs[1], outs[2:]
    gp, outs = outs[: others - 1], outs[others - 1 :]
    sums, (fs, slope) = outs[:members], outs[members:]
    first, second = mixed_pairs(length, members)
    one = lax.ppermute(one, ("blk", "grp"), first)
    two = lax.ppermute(two, ("blk", "grp"), second)
    back_x = [shifted(gp[s - 2], "grp", s) for s in range(2, members)]
    back_sum = [shifted(sums[s], "grp", s) for s in range(1, members)]
    gx, g_own, g_near = call(
        functools.partial(fourth_body, others),
        [full] * 3,
        gx,
        gy,
        slope,
        fs,
        everyone,
        *slopes,
    )
    back_near = exchanged(g_near, "blk", near_pairs)
    grad_x, grad_y, row_loss = finish(
        others,
        3.0 * members * count,
        unit_x,
        scale_x,
        gx,
        *back_x,
        unit_y,
        scale_y,
        g_own,
        back_near,
        one,
        two,
        sums[0],
        *back_sum,
    )
    return (row_loss.reshape(count), grad_x, grad_y)


def solution(mesh):
    placed = (P(("blk", "grp"), None), P(("blk", "grp"), None), P(), P(), P(("blk", "grp")))
    return jax.shard_map(
        body,
        mesh=mesh,
        in_specs=placed,
        out_specs=(P(("blk", "grp")), P(("blk", "grp"), None), P(("blk", "grp"), None)),
        check_vma=False,
    )
```

```python
import functools

import jax
import jax.numpy as jnp
from jax import lax
from jax.experimental import pallas as pl
from jax.experimental.pallas import tpu as pltpu
from jax.sharding import PartitionSpec as P


BF = jnp.bfloat16
F32 = jnp.float32
VMEM = pl.BlockSpec(memory_space=pltpu.VMEM)
SMEM = pl.BlockSpec(memory_space=pltpu.SMEM)
HBM = pl.BlockSpec(memory_space=pltpu.HBM)
CHUNKS = 4
NT = ((1,), (1,))
NN = ((1,), (0,))


def exchanged(x, axis, pairs):
    return lax.ppermute(x, axis, pairs + [(b, a) for (a, b) in pairs])


def mixed_pairs(length, members):
    first, second = [], []
    for b in range(length):
        far = (b + 1) % length if b % 2 else (b - 1) % length
        for g in range(members):
            here = b * members + g
            across = (here, far * members + g)
            along = (here, b * members + (g + 1) % members)
            direct = length % 4 == 0 and b % 4 in (1, 2)
            first.append(across if direct else along)
            second.append(along if direct else across)
    return first, second


def far_goes_first():
    place = lax.axis_index("blk")
    return (lax.axis_size("blk") % 4 == 0) & (lax.rem(place + 1, 4) >= 2)


def shifted(x, axis, by):
    length = lax.axis_size(axis)
    return lax.ppermute(x, axis, [(i, (i + by) % length) for i in range(length)])


def stacked(v):
    high = v.astype(BF)
    return jnp.concatenate([high, (v - high.astype(F32)).astype(BF)], axis=0)


def mm(a, b, dims):
    rows = a.shape[0] // 2
    deep = b.shape[0] // 2

    def one(p, q):
        return lax.dot_general(p, q, (dims, ((), ())), preferred_element_type=F32)

    both = one(a[...], b[:deep])
    return both[:rows] + (both[rows:] + one(a[:rows], b[deep:]))


def log_one_plus(t):
    series = t * (1.0 + t * (-0.5 + t * (1.0 / 3.0 + t * (-0.25 + t * 0.2))))
    return jnp.where(t < 0.03125, series, jnp.log(1.0 + t))


def gated(z, weight, diagonal=None):
    signed = z if diagonal is None else jnp.where(diagonal, -z, z)
    small = jnp.exp(-jnp.abs(signed))
    loss = jnp.maximum(signed, 0.0) + log_one_plus(small)
    slope = jnp.where(signed >= 0.0, 1.0, small) / (1.0 + small) * weight
    if diagonal is not None:
        slope = jnp.where(diagonal, -slope, slope)
    return loss, slope


def scale_of(raw):
    return lax.rsqrt(jnp.sum(raw * raw, axis=1, keepdims=True) + 1e-06)


def square(count):
    rows = lax.broadcasted_iota(jnp.int32, (count, count), 0)
    return rows == lax.broadcasted_iota(jnp.int32, (count, count), 1)


def scalars_of(tb_ref):
    return tb_ref[0:1, 0:1], tb_ref[1:2, 0:1]


def first_body(lt, bi, x_any, y_any, near_ref, w_ref, *refs):
    tb_ref, x_ref, xc_ref, y_ref, yc_ref, xs_ref, ys_ref, gx_ref, gy_ref, sum_ref = refs[:10]
    sem = refs[10]
    copies = [
        pltpu.make_async_copy(x_any, x_ref, sem.at[0]),
        pltpu.make_async_copy(y_any, y_ref, sem.at[1]),
    ]
    for copy in copies:
        copy.start()
    count = near_ref.shape[0]
    near = near_ref[...] * scale_of(near_ref[...])
    for copy, ref, scale_ref in zip(copies, (x_ref, y_ref), (xc_ref, yc_ref)):
        copy.wait()
        scale_ref[...] = scale_of(ref[...])
        ref[...] = ref[...] * scale_ref[...]
    xs_ref[...] = stacked(x_ref[...])
    ys_ref[...] = stacked(jnp.concatenate([y_ref[...], near], axis=0))
    tb_ref[0:1, :] = jnp.exp(jnp.full((1, count), lt[0], F32))
    tb_ref[1:2, :] = jnp.full((1, count), bi[0], F32)
    temper, bias = scalars_of(tb_ref)
    rows = lax.broadcasted_iota(jnp.int32, (2 * count, count), 0)
    cols = lax.broadcasted_iota(jnp.int32, (2 * count, count), 1)
    z = temper * mm(ys_ref, xs_ref, NT) + bias
    loss, slope = gated(z, w_ref[...] * temper, rows == cols)
    sum_ref[...] = jnp.sum(loss, axis=0, keepdims=True)
    gx_ref[...] = mm(stacked(slope.T), ys_ref, NN)
    gy_ref[...] = mm(stacked(slope), xs_ref, NN)


def second_body(others, tb_ref, *refs):
    raw_refs, refs = refs[:others], refs[others:]
    w_refs, refs = refs[:others], refs[others:]
    xs_ref, ys_ref, gy_in, all_ref, gnear_ref, refs = *refs[:5], refs[5:]
    gp_refs, refs = refs[:others], refs[others:]
    sump_refs, slope_refs = refs[:others], refs[others:]
    temper, bias = scalars_of(tb_ref)
    count = raw_refs[0].shape[0]
    deep = (others + 1) * count
    eye = square(count)
    all_ref[:count] = xs_ref[:count]
    all_ref[deep : deep + count] = xs_ref[count:]
    near = gy_in[count:]
    for s in range(others):
        raw = raw_refs[s][...]
        px = stacked(raw * scale_of(raw))
        here = (s + 1) * count
        all_ref[here : here + count] = px[:count]
        all_ref[deep + here : deep + here + count] = px[count:]
        z = temper * mm(px, ys_ref, NT) + bias
        weight = jnp.sum(jnp.where(eye, w_refs[s][...], 0.0), axis=1, keepdims=True)
        loss, slope = gated(z, weight * temper)
        sums = jnp.sum(loss, axis=1, keepdims=True)
        sump_refs[s][...] = jnp.sum(jnp.where(eye, sums, 0.0), axis=0, keepdims=True)
        slope_refs[s][...] = slope[:, :count]
        near = near + mm(stacked(slope[:, count:].T), px, NN)
        gp_refs[s][...] = mm(stacked(slope), ys_ref, NN)
    gnear_ref[...] = near


def third_body(others, tb_ref, *refs):
    members = others + 1
    far_ref, refs = refs[0], refs[1:]
    w_refs, refs = refs[:members], refs[members:]
    all_ref, refs = refs[0], refs[1:]
    gp_in, refs = refs[:others], refs[others:]
    sum_in, refs = refs[:members], refs[members:]
    one_ref, two_ref, refs = *refs[:2], refs[2:]
    gp_refs, refs = refs[: others - 1], refs[others - 1 :]
    sum_refs, refs = refs[:members], refs[members:]
    fs_ref, slope_ref, both_ref, turned_ref = refs
    temper, bias = scalars_of(tb_ref)
    count = far_ref.shape[0]
    far = far_ref[...]
    fs_ref[...] = stacked(far)
    scale = scale_of(far)
    z = (temper * scale) * mm(fs_ref, all_ref, NT) + bias
    weight = jnp.concatenate([w[...] for w in w_refs], axis=1) * temper
    loss, slope = gated(z, weight)
    both_ref[...] = stacked(slope)
    slope = slope * scale
    sums = jnp.sum(loss, axis=0, keepdims=True)
    for s in range(members):
        part = slice(s * count, (s + 1) * count)
        sum_refs[s][...] = sum_in[s][...] + sums[:, part]
        if s == 0:
            slope_ref[...] = slope[:, part]
        else:
            turned_ref[s - 1] = stacked(slope[:, part].T)
            if s > 1:
                gp_refs[s - 2][...] = gp_in[s - 1][...] + mm(turned_ref[s - 1], fs_ref, NN)

    def finish_into(far_out, next_out):
        far_out[...] = mm(both_ref, all_ref, NN)
        next_out[...] = gp_in[0][...] + mm(turned_ref[0], fs_ref, NN)

    far_first = far_goes_first()
    pl.when(far_first)(lambda: finish_into(one_ref, two_ref))
    pl.when(jnp.logical_not(far_first))(lambda: finish_into(two_ref, one_ref))


def fourth_body(others, gx_in, gy_in, slope_ref, fs_ref, all_ref, *refs):
    slopes, (gx_ref, gown_ref) = refs[:others], refs[others:]
    count = gx_in.shape[0]
    deep = (others + 1) * count
    gy = gy_in[:count]
    for s in range(others):
        here = (s + 1) * count
        px = jnp.concatenate(
            [all_ref[here : here + count], all_ref[deep + here : deep + here + count]], axis=0
        )
        gy = gy + mm(stacked(slopes[s][...].T), px, NN)
    gown_ref[...] = gy
    gx_ref[...] = gx_in[...] + mm(stacked(slope_ref[...].T), fs_ref, NN)


def last_body(others, pairs, *refs):
    (unit_x, scale_x, own_x), refs = refs[:3], refs[3:]
    back_x, refs = refs[: others - 1], refs[others - 1 :]
    (unit_y, scale_y, own_y, near_y, one, two), refs = refs[:6], refs[6:]
    sums, refs = refs[: others + 1], refs[others + 1 :]
    x_out, y_out, loss_out, held, line, sem = refs
    rows = unit_x.shape[0] // CHUNKS
    total = sums[0][...]
    for r in sums[1:]:
        total = total + r[...]
    line[...] = total / pairs

    def run(far_y, next_x):
        copies = []

        def send(source, target):
            copies.append(pltpu.make_async_copy(source, target, sem.at[len(copies)]))
            copies[-1].start()

        send(line, loss_out)
        sides = [
            (unit_x, scale_x, [own_x, next_x, *back_x], x_out),
            (unit_y, scale_y, [own_y, near_y, far_y], y_out),
        ]
        for k, (unit_ref, scale_ref, grads, out_ref) in enumerate(sides):
            for c in range(CHUNKS):
                here = pl.ds(c * rows, rows)
                grad = grads[0][here, :]
                for r in grads[1:]:
                    grad = grad + r[here, :]
                unit = unit_ref[here, :]
                inner = jnp.sum(unit * grad, axis=1, keepdims=True)
                held[k, here, :] = scale_ref[here, :] * (grad - unit * inner)
                send(held.at[k, here, :], out_ref.at[here, :])
        for copy in copies:
            copy.wait()

    far_first = far_goes_first()
    pl.when(far_first)(lambda: run(one, two))
    pl.when(jnp.logical_not(far_first))(lambda: run(two, one))


def shape(*dims, kind=F32):
    return jax.ShapeDtypeStruct(dims, kind)


PARAMS = pltpu.CompilerParams(vmem_limit_bytes=16 * 1024 * 1024)


def in_hbm(args):
    return [pltpu.with_memory_space_constraint(a, pltpu.HBM) for a in args]


def in_vmem(args):
    return [pltpu.with_memory_space_constraint(a, pltpu.VMEM) for a in args]


def call(body, outs, *args, scratch=(), scalars=0, anywhere=0):
    numbers, args = args[:scalars], args[scalars:]
    return pl.pallas_call(
        body,
        out_shape=[pltpu.VMEM(o.shape, o.dtype) for o in outs],
        in_specs=[SMEM] * scalars + [HBM] * anywhere + [VMEM] * (len(args) - anywhere),
        out_specs=[VMEM] * len(outs),
        scratch_shapes=list(scratch),
        compiler_params=PARAMS,
    )(*numbers, *in_hbm(args[:anywhere]), *in_vmem(args[anywhere:]))


def finish(others, pairs, *args):
    full = shape(*args[0].shape)
    line = shape(1, full.shape[0])
    return pl.pallas_call(
        functools.partial(last_body, others, pairs),
        out_shape=[full, full, line],
        in_specs=[VMEM] * len(args),
        out_specs=[HBM] * 3,
        scratch_shapes=[
            pltpu.VMEM((2, *full.shape), F32),
            pltpu.VMEM(line.shape, F32),
            pltpu.SemaphoreType.DMA((2 * CHUNKS + 1,)),
        ],
        compiler_params=PARAMS,
    )(*in_vmem(args))


def body(images, texts, log_temp, bias, row_weight):
    members = lax.axis_size("grp")
    others = members - 1
    count, width = images.shape
    weight = row_weight.reshape(1, count)
    length = lax.axis_size("blk")
    near_pairs = [(i, i + 1) for i in range(0, length, 2)]
    far_pairs = [(i, (i + 1) % length) for i in range(1, length, 2)]
    raws = [shifted(images, "grp", -s) for s in range(1, members)]
    far = exchanged(texts, "blk", far_pairs)
    near = exchanged(texts, "blk", near_pairs)
    weights = [weight] + [shifted(weight, "grp", -s) for s in range(1, members)]
    full = shape(count, width)
    line = shape(1, count)
    stack = shape(2 * count, width, kind=BF)
    tb, unit_x, scale_x, unit_y, scale_y, xs, ys, gx, gy, sums = call(
        first_body,
        [
            shape(2, count),
            full,
            shape(count, 1),
            full,
            shape(count, 1),
            stack,
            shape(4 * count, width, kind=BF),
            full,
            shape(2 * count, width),
            line,
        ],
        log_temp,
        bias,
        images,
        texts,
        near,
        weight,
        scratch=[pltpu.SemaphoreType.DMA((2,))],
        scalars=2,
        anywhere=2,
    )
    outs = call(
        functools.partial(second_body, others),
        [shape(2 * members * count, width, kind=BF), full]
        + [full] * others
        + [line] * others
        + [shape(count, count)] * others,
        tb,
        *raws,
        *weights[1:],
        xs,
        ys,
        gy,
    )
    everyone, g_near, outs = outs[0], outs[1], outs[2:]
    gp, outs = outs[:others], outs[others:]
    sump, slopes = outs[:others], outs[others:]
    back_near = exchanged(g_near, "blk", near_pairs)
    outs = call(
        functools.partial(third_body, others),
        [full, full]
        + [full] * (others - 1)
        + [line] * members
        + [stack, shape(count, count)],
        tb,
        far,
        *weights,
        everyone,
        *gp,
        sums,
        *sump,
        scratch=[
            pltpu.VMEM((2 * count, members * count), BF),
            pltpu.VMEM((others, 2 * count, count), BF),
        ],
    )
    one, two, outs = outs[0], outs[1], outs[2:]
    gp, outs = outs[: others - 1], outs[others - 1 :]
    sums, (fs, slope) = outs[:members], outs[members:]
    first, second = mixed_pairs(length, members)
    one = lax.ppermute(one, ("blk", "grp"), first)
    two = lax.ppermute(two, ("blk", "grp"), second)
    back_x = [shifted(gp[s - 2], "grp", s) for s in range(2, members)]
    back_sum = [shifted(sums[s], "grp", s) for s in range(1, members)]
    gx, g_own = call(
        functools.partial(fourth_body, others),
        [full] * 2,
        gx,
        gy,
        slope,
        fs,
        everyone,
        *slopes,
    )
    grad_x, grad_y, row_loss = finish(
        others,
        3.0 * members * count,
        unit_x,
        scale_x,
        gx,
        *back_x,
        unit_y,
        scale_y,
        g_own,
        back_near,
        one,
        two,
        sums[0],
        *back_sum,
    )
    return (row_loss.reshape(count), grad_x, grad_y)


def solution(mesh):
    placed = (P(("blk", "grp"), None), P(("blk", "grp"), None), P(), P(), P(("blk", "grp")))
    return jax.shard_map(
        body,
        mesh=mesh,
        in_specs=placed,
        out_specs=(P(("blk", "grp")), P(("blk", "grp"), None), P(("blk", "grp"), None)),
        check_vma=False,
    )
```

```python
import functools

import jax
import jax.numpy as jnp
from jax import lax
from jax.experimental import pallas as pl
from jax.experimental.pallas import tpu as pltpu
from jax.sharding import PartitionSpec as P


BF = jnp.bfloat16
F32 = jnp.float32
VMEM = pl.BlockSpec(memory_space=pltpu.VMEM)
SMEM = pl.BlockSpec(memory_space=pltpu.SMEM)
HBM = pl.BlockSpec(memory_space=pltpu.HBM)
CHUNKS = 4
NT = ((1,), (1,))
NN = ((1,), (0,))


def exchanged(x, axis, pairs):
    return lax.ppermute(x, axis, pairs + [(b, a) for (a, b) in pairs])


def mixed_pairs(length, members):
    first, second = [], []
    for b in range(length):
        far = (b + 1) % length if b % 2 else (b - 1) % length
        for g in range(members):
            here = b * members + g
            across = (here, far * members + g)
            along = (here, b * members + (g + 1) % members)
            direct = length % 4 == 0 and b % 4 in (1, 2)
            first.append(across if direct else along)
            second.append(along if direct else across)
    return first, second


def far_goes_first():
    place = lax.axis_index("blk")
    return (lax.axis_size("blk") % 4 == 0) & (lax.rem(place + 1, 4) >= 2)


def shifted(x, axis, by):
    length = lax.axis_size(axis)
    return lax.ppermute(x, axis, [(i, (i + by) % length) for i in range(length)])


def stacked(v):
    high = v.astype(BF)
    return jnp.concatenate([high, (v - high.astype(F32)).astype(BF)], axis=0)


def mm(a, b, dims):
    rows = a.shape[0] // 2
    deep = b.shape[0] // 2

    def one(p, q):
        return lax.dot_general(p, q, (dims, ((), ())), preferred_element_type=F32)

    both = one(a[...], b[:deep])
    return both[:rows] + (both[rows:] + one(a[:rows], b[deep:]))


def log_one_plus(t):
    series = t * (1.0 + t * (-0.5 + t * (1.0 / 3.0 + t * (-0.25 + t * 0.2))))
    return jnp.where(t < 0.03125, series, jnp.log(1.0 + t))


def gated(z, weight, diagonal=None):
    signed = z if diagonal is None else jnp.where(diagonal, -z, z)
    small = jnp.exp(-jnp.abs(signed))
    loss = jnp.maximum(signed, 0.0) + log_one_plus(small)
    slope = jnp.where(signed >= 0.0, 1.0, small) / (1.0 + small) * weight
    if diagonal is not None:
        slope = jnp.where(diagonal, -slope, slope)
    return loss, slope


def scale_of(raw):
    return lax.rsqrt(jnp.sum(raw * raw, axis=1, keepdims=True) + 1e-06)


def square(count):
    rows = lax.broadcasted_iota(jnp.int32, (count, count), 0)
    return rows == lax.broadcasted_iota(jnp.int32, (count, count), 1)


def scalars_of(tb_ref):
    return tb_ref[0:1, 0:1], tb_ref[1:2, 0:1]


def first_body(lt, bi, x_any, y_any, near_ref, w_ref, *refs):
    tb_ref, x_ref, xc_ref, y_ref, yc_ref, xs_ref, ys_ref, gx_ref, gy_ref, sum_ref = refs[:10]
    sem = refs[10]
    copies = [
        pltpu.make_async_copy(x_any, x_ref, sem.at[0]),
        pltpu.make_async_copy(y_any, y_ref, sem.at[1]),
    ]
    for copy in copies:
        copy.start()
    count = near_ref.shape[0]
    near = near_ref[...] * scale_of(near_ref[...])
    for copy, ref, scale_ref in zip(copies, (x_ref, y_ref), (xc_ref, yc_ref)):
        copy.wait()
        scale_ref[...] = scale_of(ref[...])
        ref[...] = ref[...] * scale_ref[...]
    xs_ref[...] = stacked(x_ref[...])
    ys_ref[...] = stacked(jnp.concatenate([y_ref[...], near], axis=0))
    tb_ref[0:1, :] = jnp.exp(jnp.full((1, count), lt[0], F32))
    tb_ref[1:2, :] = jnp.full((1, count), bi[0], F32)
    temper, bias = scalars_of(tb_ref)
    rows = lax.broadcasted_iota(jnp.int32, (2 * count, count), 0)
    cols = lax.broadcasted_iota(jnp.int32, (2 * count, count), 1)
    z = temper * mm(ys_ref, xs_ref, NT) + bias
    loss, slope = gated(z, w_ref[...] * temper, rows == cols)
    sum_ref[...] = jnp.sum(loss, axis=0, keepdims=True)
    gx_ref[...] = mm(stacked(slope.T), ys_ref, NN)
    gy_ref[...] = mm(stacked(slope), xs_ref, NN)


def second_body(others, tb_ref, *refs):
    raw_refs, refs = refs[:others], refs[others:]
    w_refs, refs = refs[:others], refs[others:]
    xs_ref, ys_ref, all_ref, refs = *refs[:3], refs[3:]
    gp_refs, refs = refs[:others], refs[others:]
    sump_refs, slope_refs = refs[:others], refs[others:]
    temper, bias = scalars_of(tb_ref)
    count = raw_refs[0].shape[0]
    deep = (others + 1) * count
    eye = square(count)
    all_ref[:count] = xs_ref[:count]
    all_ref[deep : deep + count] = xs_ref[count:]
    for s in range(others):
        raw = raw_refs[s][...]
        px = stacked(raw * scale_of(raw))
        here = (s + 1) * count
        all_ref[here : here + count] = px[:count]
        all_ref[deep + here : deep + here + count] = px[count:]
        z = temper * mm(px, ys_ref, NT) + bias
        weight = jnp.sum(jnp.where(eye, w_refs[s][...], 0.0), axis=1, keepdims=True)
        loss, slope = gated(z, weight * temper)
        sums = jnp.sum(loss, axis=1, keepdims=True)
        sump_refs[s][...] = jnp.sum(jnp.where(eye, sums, 0.0), axis=0, keepdims=True)
        slope_refs[s][...] = slope
        gp_refs[s][...] = mm(stacked(slope), ys_ref, NN)


def third_body(others, tb_ref, *refs):
    members = others + 1
    far_ref, refs = refs[0], refs[1:]
    w_refs, refs = refs[:members], refs[members:]
    all_ref, gp_in, refs = *refs[:2], refs[2:]
    sum_in, refs = refs[:members], refs[members:]
    one_ref, refs = refs[0], refs[1:]
    sum_refs, refs = refs[:members], refs[members:]
    fs_ref, both_ref, slope_ref = refs
    temper, bias = scalars_of(tb_ref)
    count = far_ref.shape[0]
    far = far_ref[...]
    fs_ref[...] = stacked(far)
    scale = scale_of(far)
    z = (temper * scale) * mm(fs_ref, all_ref, NT) + bias
    weight = jnp.concatenate([w[...] for w in w_refs], axis=1) * temper
    loss, slope = gated(z, weight)
    both_ref[...] = stacked(slope)
    slope = slope * scale
    sums = jnp.sum(loss, axis=0, keepdims=True)
    for s in range(members):
        part = slice(s * count, (s + 1) * count)
        sum_refs[s][...] = sum_in[s][...] + sums[:, part]
        slope_ref[s] = slope[:, part]

    @pl.when(far_goes_first())
    def _():
        one_ref[...] = mm(both_ref, all_ref, NN)

    @pl.when(jnp.logical_not(far_goes_first()))
    def _():
        one_ref[...] = gp_in[...] + mm(stacked(slope_ref[1].T), fs_ref, NN)


def rest_body(others, *refs):
    gp_in, (fs_ref, both_ref, slope_ref, all_ref, two_ref), gp_refs = (
        refs[:others],
        refs[others : others + 5],
        refs[others + 5 :],
    )

    @pl.when(far_goes_first())
    def _():
        two_ref[...] = gp_in[0][...] + mm(stacked(slope_ref[1].T), fs_ref, NN)

    @pl.when(jnp.logical_not(far_goes_first()))
    def _():
        two_ref[...] = mm(both_ref, all_ref, NN)

    for s in range(2, others + 1):
        gp_refs[s - 2][...] = gp_in[s - 1][...] + mm(stacked(slope_ref[s].T), fs_ref, NN)


def fourth_body(others, gx_in, gy_in, slope_ref, fs_ref, all_ref, *refs):
    slopes, (gx_ref, gown_ref, gnear_ref) = refs[:others], refs[others:]
    count = gx_in.shape[0]
    deep = (others + 1) * count
    gy = gy_in[...]
    for s in range(others):
        here = (s + 1) * count
        px = jnp.concatenate(
            [all_ref[here : here + count], all_ref[deep + here : deep + here + count]], axis=0
        )
        gy = gy + mm(stacked(slopes[s][...].T), px, NN)
    gown_ref[...] = gy[:count]
    gnear_ref[...] = gy[count:]
    gx_ref[...] = gx_in[...] + mm(stacked(slope_ref[0].T), fs_ref, NN)


def last_body(others, pairs, *refs):
    (unit_x, scale_x, own_x), refs = refs[:3], refs[3:]
    back_x, refs = refs[: others - 1], refs[others - 1 :]
    (unit_y, scale_y, own_y, near_y, one, two), refs = refs[:6], refs[6:]
    sums, refs = refs[: others + 1], refs[others + 1 :]
    x_out, y_out, loss_out, held, line, sem = refs
    rows = unit_x.shape[0] // CHUNKS
    total = sums[0][...]
    for r in sums[1:]:
        total = total + r[...]
    line[...] = total / pairs

    def run(far_y, next_x):
        copies = []

        def send(source, target):
            copies.append(pltpu.make_async_copy(source, target, sem.at[len(copies)]))
            copies[-1].start()

        send(line, loss_out)
        sides = [
            (unit_x, scale_x, [own_x, next_x, *back_x], x_out),
            (unit_y, scale_y, [own_y, near_y, far_y], y_out),
        ]
        for k, (unit_ref, scale_ref, grads, out_ref) in enumerate(sides):
            for c in range(CHUNKS):
                here = pl.ds(c * rows, rows)
                grad = grads[0][here, :]
                for r in grads[1:]:
                    grad = grad + r[here, :]
                unit = unit_ref[here, :]
                inner = jnp.sum(unit * grad, axis=1, keepdims=True)
                held[k, here, :] = scale_ref[here, :] * (grad - unit * inner)
                send(held.at[k, here, :], out_ref.at[here, :])
        for copy in copies:
            copy.wait()

    far_first = far_goes_first()
    pl.when(far_first)(lambda: run(one, two))
    pl.when(jnp.logical_not(far_first))(lambda: run(two, one))


def shape(*dims, kind=F32):
    return jax.ShapeDtypeStruct(dims, kind)


PARAMS = pltpu.CompilerParams(vmem_limit_bytes=16 * 1024 * 1024)


def in_hbm(args):
    return [pltpu.with_memory_space_constraint(a, pltpu.HBM) for a in args]


def in_vmem(args):
    return [pltpu.with_memory_space_constraint(a, pltpu.VMEM) for a in args]


def call(body, outs, *args, scratch=(), scalars=0, anywhere=0):
    numbers, args = args[:scalars], args[scalars:]
    return pl.pallas_call(
        body,
        out_shape=[pltpu.VMEM(o.shape, o.dtype) for o in outs],
        in_specs=[SMEM] * scalars + [HBM] * anywhere + [VMEM] * (len(args) - anywhere),
        out_specs=[VMEM] * len(outs),
        scratch_shapes=list(scratch),
        compiler_params=PARAMS,
    )(*numbers, *in_hbm(args[:anywhere]), *in_vmem(args[anywhere:]))


def finish(others, pairs, *args):
    full = shape(*args[0].shape)
    line = shape(1, full.shape[0])
    return pl.pallas_call(
        functools.partial(last_body, others, pairs),
        out_shape=[full, full, line],
        in_specs=[VMEM] * len(args),
        out_specs=[HBM] * 3,
        scratch_shapes=[
            pltpu.VMEM((2, *full.shape), F32),
            pltpu.VMEM(line.shape, F32),
            pltpu.SemaphoreType.DMA((2 * CHUNKS + 1,)),
        ],
        compiler_params=PARAMS,
    )(*in_vmem(args))


def body(images, texts, log_temp, bias, row_weight):
    members = lax.axis_size("grp")
    others = members - 1
    count, width = images.shape
    weight = row_weight.reshape(1, count)
    length = lax.axis_size("blk")
    near_pairs = [(i, i + 1) for i in range(0, length, 2)]
    far_pairs = [(i, (i + 1) % length) for i in range(1, length, 2)]
    raws = [shifted(images, "grp", -s) for s in range(1, members)]
    far = exchanged(texts, "blk", far_pairs)
    near = exchanged(texts, "blk", near_pairs)
    weights = [weight] + [shifted(weight, "grp", -s) for s in range(1, members)]
    full = shape(count, width)
    line = shape(1, count)
    stack = shape(2 * count, width, kind=BF)
    tb, unit_x, scale_x, unit_y, scale_y, xs, ys, gx, gy, sums = call(
        first_body,
        [
            shape(2, count),
            full,
            shape(count, 1),
            full,
            shape(count, 1),
            stack,
            shape(4 * count, width, kind=BF),
            full,
            shape(2 * count, width),
            line,
        ],
        log_temp,
        bias,
        images,
        texts,
        near,
        weight,
        scratch=[pltpu.SemaphoreType.DMA((2,))],
        scalars=2,
        anywhere=2,
    )
    outs = call(
        functools.partial(second_body, others),
        [shape(2 * members * count, width, kind=BF)]
        + [full] * others
        + [line] * others
        + [shape(count, 2 * count)] * others,
        tb,
        *raws,
        *weights[1:],
        xs,
        ys,
    )
    everyone, outs = outs[0], outs[1:]
    gp, outs = outs[:others], outs[others:]
    sump, slopes = outs[:others], outs[others:]
    outs = call(
        functools.partial(third_body, others),
        [full]
        + [line] * members
        + [
            stack,
            shape(2 * count, members * count, kind=BF),
            shape(members, count, count),
        ],
        tb,
        far,
        *weights,
        everyone,
        gp[0],
        sums,
        *sump,
    )
    one, outs = outs[0], outs[1:]
    sums, (fs, both, slope) = outs[:members], outs[members:]
    first, second = mixed_pairs(length, members)
    one = lax.ppermute(one, ("blk", "grp"), first)
    two, *gp = call(
        functools.partial(rest_body, others),
        [full] * others,
        *gp,
        fs,
        both,
        slope,
        everyone,
    )
    two = lax.ppermute(two, ("blk", "grp"), second)
    back_x = [shifted(gp[s - 2], "grp", s) for s in range(2, members)]
    back_sum = [shifted(sums[s], "grp", s) for s in range(1, members)]
    gx, g_own, g_near = call(
        functools.partial(fourth_body, others),
        [full] * 3,
        gx,
        gy,
        slope,
        fs,
        everyone,
        *slopes,
    )
    back_near = exchanged(g_near, "blk", near_pairs)
    grad_x, grad_y, row_loss = finish(
        others,
        3.0 * members * count,
        unit_x,
        scale_x,
        gx,
        *back_x,
        unit_y,
        scale_y,
        g_own,
        back_near,
        one,
        two,
        sums[0],
        *back_sum,
    )
    return (row_loss.reshape(count), grad_x, grad_y)


def solution(mesh):
    placed = (P(("blk", "grp"), None), P(("blk", "grp"), None), P(), P(), P(("blk", "grp")))
    return jax.shard_map(
        body,
        mesh=mesh,
        in_specs=placed,
        out_specs=(P(("blk", "grp")), P(("blk", "grp"), None), P(("blk", "grp"), None)),
        check_vma=False,
    )
```

```python
import functools

import jax
import jax.numpy as jnp
from jax import lax
from jax.experimental import pallas as pl
from jax.experimental.pallas import tpu as pltpu
from jax.sharding import PartitionSpec as P


BF = jnp.bfloat16
F32 = jnp.float32
VMEM = pl.BlockSpec(memory_space=pltpu.VMEM)
SMEM = pl.BlockSpec(memory_space=pltpu.SMEM)
HBM = pl.BlockSpec(memory_space=pltpu.HBM)
CHUNKS = 4
NT = ((1,), (1,))
NN = ((1,), (0,))


def exchanged(x, axis, pairs):
    return lax.ppermute(x, axis, pairs + [(b, a) for (a, b) in pairs])


def mixed_pairs(length, members):
    first, second = [], []
    for b in range(length):
        far = (b + 1) % length if b % 2 else (b - 1) % length
        for g in range(members):
            here = b * members + g
            across = (here, far * members + g)
            along = (here, b * members + (g + 1) % members)
            end = b in (0, length - 1)
            direct = length % 4 == 0 and (end or (b % 4 in (1, 2) and 2 < b < length - 3))
            first.append(across if direct else along)
            second.append(along if direct else across)
    return first, second


def far_goes_first():
    place = lax.axis_index("blk")
    length = lax.axis_size("blk")
    end = (place == 0) | (place == length - 1)
    inner = (place > 2) & (place < length - 3) & (lax.rem(place + 1, 4) >= 2)
    return (length % 4 == 0) & (end | inner)


def shifted(x, axis, by):
    length = lax.axis_size(axis)
    return lax.ppermute(x, axis, [(i, (i + by) % length) for i in range(length)])


def stacked(v):
    high = v.astype(BF)
    return jnp.concatenate([high, (v - high.astype(F32)).astype(BF)], axis=0)


def mm(a, b, dims):
    rows = a.shape[0] // 2
    deep = b.shape[0] // 2

    def one(p, q):
        return lax.dot_general(p, q, (dims, ((), ())), preferred_element_type=F32)

    both = one(a[...], b[:deep])
    return both[:rows] + (both[rows:] + one(a[:rows], b[deep:]))


def log_one_plus(t):
    series = t * (1.0 + t * (-0.5 + t * (1.0 / 3.0 + t * (-0.25 + t * 0.2))))
    return jnp.where(t < 0.03125, series, jnp.log(1.0 + t))


def gated(z, weight, diagonal=None):
    signed = z if diagonal is None else jnp.where(diagonal, -z, z)
    small = jnp.exp(-jnp.abs(signed))
    loss = jnp.maximum(signed, 0.0) + log_one_plus(small)
    slope = jnp.where(signed >= 0.0, 1.0, small) / (1.0 + small) * weight
    if diagonal is not None:
        slope = jnp.where(diagonal, -slope, slope)
    return loss, slope


def scale_of(raw):
    return lax.rsqrt(jnp.sum(raw * raw, axis=1, keepdims=True) + 1e-06)


def square(count):
    rows = lax.broadcasted_iota(jnp.int32, (count, count), 0)
    return rows == lax.broadcasted_iota(jnp.int32, (count, count), 1)


def scalars_of(tb_ref):
    return tb_ref[0:1, 0:1], tb_ref[1:2, 0:1]


def first_body(lt, bi, x_any, y_any, near_ref, w_ref, *refs):
    tb_ref, x_ref, xc_ref, y_ref, yc_ref, xs_ref, ys_ref, gx_ref, gy_ref, sum_ref = refs[:10]
    sem = refs[10]
    copies = [
        pltpu.make_async_copy(x_any, x_ref, sem.at[0]),
        pltpu.make_async_copy(y_any, y_ref, sem.at[1]),
    ]
    for copy in copies:
        copy.start()
    count = near_ref.shape[0]
    near = near_ref[...] * scale_of(near_ref[...])
    for copy, ref, scale_ref in zip(copies, (x_ref, y_ref), (xc_ref, yc_ref)):
        copy.wait()
        scale_ref[...] = scale_of(ref[...])
        ref[...] = ref[...] * scale_ref[...]
    xs_ref[...] = stacked(x_ref[...])
    ys_ref[...] = stacked(jnp.concatenate([y_ref[...], near], axis=0))
    tb_ref[0:1, :] = jnp.exp(jnp.full((1, count), lt[0], F32))
    tb_ref[1:2, :] = jnp.full((1, count), bi[0], F32)
    temper, bias = scalars_of(tb_ref)
    rows = lax.broadcasted_iota(jnp.int32, (2 * count, count), 0)
    cols = lax.broadcasted_iota(jnp.int32, (2 * count, count), 1)
    z = temper * mm(ys_ref, xs_ref, NT) + bias
    loss, slope = gated(z, w_ref[...] * temper, rows == cols)
    sum_ref[...] = jnp.sum(loss, axis=0, keepdims=True)
    gx_ref[...] = mm(stacked(slope.T), ys_ref, NN)
    gy_ref[...] = mm(stacked(slope), xs_ref, NN)


def second_body(others, tb_ref, *refs):
    raw_refs, refs = refs[:others], refs[others:]
    w_refs, refs = refs[:others], refs[others:]
    xs_ref, ys_ref, all_ref, refs = *refs[:3], refs[3:]
    gp_refs, refs = refs[:others], refs[others:]
    sump_refs, slope_refs = refs[:others], refs[others:]
    temper, bias = scalars_of(tb_ref)
    count = raw_refs[0].shape[0]
    deep = (others + 1) * count
    eye = square(count)
    all_ref[:count] = xs_ref[:count]
    all_ref[deep : deep + count] = xs_ref[count:]
    for s in range(others):
        raw = raw_refs[s][...]
        px = stacked(raw * scale_of(raw))
        here = (s + 1) * count
        all_ref[here : here + count] = px[:count]
        all_ref[deep + here : deep + here + count] = px[count:]
        z = temper * mm(px, ys_ref, NT) + bias
        weight = jnp.sum(jnp.where(eye, w_refs[s][...], 0.0), axis=1, keepdims=True)
        loss, slope = gated(z, weight * temper)
        sums = jnp.sum(loss, axis=1, keepdims=True)
        sump_refs[s][...] = jnp.sum(jnp.where(eye, sums, 0.0), axis=0, keepdims=True)
        slope_refs[s][...] = slope
        gp_refs[s][...] = mm(stacked(slope), ys_ref, NN)


def third_body(others, tb_ref, *refs):
    members = others + 1
    far_ref, refs = refs[0], refs[1:]
    w_refs, refs = refs[:members], refs[members:]
    all_ref, gp_in, refs = *refs[:2], refs[2:]
    sum_in, refs = refs[:members], refs[members:]
    one_ref, refs = refs[0], refs[1:]
    sum_refs, refs = refs[:members], refs[members:]
    fs_ref, both_ref, slope_ref = refs
    temper, bias = scalars_of(tb_ref)
    count = far_ref.shape[0]
    far = far_ref[...]
    fs_ref[...] = stacked(far)
    scale = scale_of(far)
    z = (temper * scale) * mm(fs_ref, all_ref, NT) + bias
    weight = jnp.concatenate([w[...] for w in w_refs], axis=1) * temper
    loss, slope = gated(z, weight)
    both_ref[...] = stacked(slope)
    slope = slope * scale
    sums = jnp.sum(loss, axis=0, keepdims=True)
    for s in range(members):
        part = slice(s * count, (s + 1) * count)
        sum_refs[s][...] = sum_in[s][...] + sums[:, part]
        slope_ref[s] = slope[:, part]

    @pl.when(far_goes_first())
    def _():
        one_ref[...] = mm(both_ref, all_ref, NN)

    @pl.when(jnp.logical_not(far_goes_first()))
    def _():
        one_ref[...] = gp_in[...] + mm(stacked(slope_ref[1].T), fs_ref, NN)


def rest_body(others, *refs):
    gp_in, (fs_ref, both_ref, slope_ref, all_ref, two_ref), gp_refs = (
        refs[:others],
        refs[others : others + 5],
        refs[others + 5 :],
    )

    @pl.when(far_goes_first())
    def _():
        two_ref[...] = gp_in[0][...] + mm(stacked(slope_ref[1].T), fs_ref, NN)

    @pl.when(jnp.logical_not(far_goes_first()))
    def _():
        two_ref[...] = mm(both_ref, all_ref, NN)

    for s in range(2, others + 1):
        gp_refs[s - 2][...] = gp_in[s - 1][...] + mm(stacked(slope_ref[s].T), fs_ref, NN)


def fourth_body(others, gx_in, gy_in, slope_ref, fs_ref, all_ref, *refs):
    slopes, (gx_ref, gown_ref, gnear_ref) = refs[:others], refs[others:]
    count = gx_in.shape[0]
    deep = (others + 1) * count
    gy = gy_in[...]
    for s in range(others):
        here = (s + 1) * count
        px = jnp.concatenate(
            [all_ref[here : here + count], all_ref[deep + here : deep + here + count]], axis=0
        )
        gy = gy + mm(stacked(slopes[s][...].T), px, NN)
    gown_ref[...] = gy[:count]
    gnear_ref[...] = gy[count:]
    gx_ref[...] = gx_in[...] + mm(stacked(slope_ref[0].T), fs_ref, NN)


def last_body(others, pairs, *refs):
    (unit_x, scale_x, own_x), refs = refs[:3], refs[3:]
    back_x, refs = refs[: others - 1], refs[others - 1 :]
    (unit_y, scale_y, own_y, near_y, one, two), refs = refs[:6], refs[6:]
    sums, refs = refs[: others + 1], refs[others + 1 :]
    x_out, y_out, loss_out, held, line, sem = refs
    rows = unit_x.shape[0] // CHUNKS
    total = sums[0][...]
    for r in sums[1:]:
        total = total + r[...]
    line[...] = total / pairs

    def run(far_y, next_x):
        copies = []

        def send(source, target):
            copies.append(pltpu.make_async_copy(source, target, sem.at[len(copies)]))
            copies[-1].start()

        send(line, loss_out)
        sides = [
            (unit_x, scale_x, [own_x, next_x, *back_x], x_out),
            (unit_y, scale_y, [own_y, near_y, far_y], y_out),
        ]
        for k, (unit_ref, scale_ref, grads, out_ref) in enumerate(sides):
            for c in range(CHUNKS):
                here = pl.ds(c * rows, rows)
                grad = grads[0][here, :]
                for r in grads[1:]:
                    grad = grad + r[here, :]
                unit = unit_ref[here, :]
                inner = jnp.sum(unit * grad, axis=1, keepdims=True)
                held[k, here, :] = scale_ref[here, :] * (grad - unit * inner)
                send(held.at[k, here, :], out_ref.at[here, :])
        for copy in copies:
            copy.wait()

    far_first = far_goes_first()
    pl.when(far_first)(lambda: run(one, two))
    pl.when(jnp.logical_not(far_first))(lambda: run(two, one))


def shape(*dims, kind=F32):
    return jax.ShapeDtypeStruct(dims, kind)


PARAMS = pltpu.CompilerParams(vmem_limit_bytes=16 * 1024 * 1024)


def in_hbm(args):
    return [pltpu.with_memory_space_constraint(a, pltpu.HBM) for a in args]


def in_vmem(args):
    return [pltpu.with_memory_space_constraint(a, pltpu.VMEM) for a in args]


def call(body, outs, *args, scratch=(), scalars=0, anywhere=0):
    numbers, args = args[:scalars], args[scalars:]
    return pl.pallas_call(
        body,
        out_shape=[pltpu.VMEM(o.shape, o.dtype) for o in outs],
        in_specs=[SMEM] * scalars + [HBM] * anywhere + [VMEM] * (len(args) - anywhere),
        out_specs=[VMEM] * len(outs),
        scratch_shapes=list(scratch),
        compiler_params=PARAMS,
    )(*numbers, *in_hbm(args[:anywhere]), *in_vmem(args[anywhere:]))


def finish(others, pairs, *args):
    full = shape(*args[0].shape)
    line = shape(1, full.shape[0])
    return pl.pallas_call(
        functools.partial(last_body, others, pairs),
        out_shape=[full, full, line],
        in_specs=[VMEM] * len(args),
        out_specs=[HBM] * 3,
        scratch_shapes=[
            pltpu.VMEM((2, *full.shape), F32),
            pltpu.VMEM(line.shape, F32),
            pltpu.SemaphoreType.DMA((2 * CHUNKS + 1,)),
        ],
        compiler_params=PARAMS,
    )(*in_vmem(args))


def body(images, texts, log_temp, bias, row_weight):
    members = lax.axis_size("grp")
    others = members - 1
    count, width = images.shape
    weight = row_weight.reshape(1, count)
    length = lax.axis_size("blk")
    near_pairs = [(i, i + 1) for i in range(0, length, 2)]
    far_pairs = [(i, (i + 1) % length) for i in range(1, length, 2)]
    raws = [shifted(images, "grp", -s) for s in range(1, members)]
    far = exchanged(texts, "blk", far_pairs)
    near = exchanged(texts, "blk", near_pairs)
    weights = [weight] + [shifted(weight, "grp", -s) for s in range(1, members)]
    full = shape(count, width)
    line = shape(1, count)
    stack = shape(2 * count, width, kind=BF)
    tb, unit_x, scale_x, unit_y, scale_y, xs, ys, gx, gy, sums = call(
        first_body,
        [
            shape(2, count),
            full,
            shape(count, 1),
            full,
            shape(count, 1),
            stack,
            shape(4 * count, width, kind=BF),
            full,
            shape(2 * count, width),
            line,
        ],
        log_temp,
        bias,
        images,
        texts,
        near,
        weight,
        scratch=[pltpu.SemaphoreType.DMA((2,))],
        scalars=2,
        anywhere=2,
    )
    outs = call(
        functools.partial(second_body, others),
        [shape(2 * members * count, width, kind=BF)]
        + [full] * others
        + [line] * others
        + [shape(count, 2 * count)] * others,
        tb,
        *raws,
        *weights[1:],
        xs,
        ys,
    )
    everyone, outs = outs[0], outs[1:]
    gp, outs = outs[:others], outs[others:]
    sump, slopes = outs[:others], outs[others:]
    outs = call(
        functools.partial(third_body, others),
        [full]
        + [line] * members
        + [
            stack,
            shape(2 * count, members * count, kind=BF),
            shape(members, count, count),
        ],
        tb,
        far,
        *weights,
        everyone,
        gp[0],
        sums,
        *sump,
    )
    one, outs = outs[0], outs[1:]
    sums, (fs, both, slope) = outs[:members], outs[members:]
    first, second = mixed_pairs(length, members)
    one = lax.ppermute(one, ("blk", "grp"), first)
    two, *gp = call(
        functools.partial(rest_body, others),
        [full] * others,
        *gp,
        fs,
        both,
        slope,
        everyone,
    )
    two = lax.ppermute(two, ("blk", "grp"), second)
    back_x = [shifted(gp[s - 2], "grp", s) for s in range(2, members)]
    back_sum = [shifted(sums[s], "grp", s) for s in range(1, members)]
    gx, g_own, g_near = call(
        functools.partial(fourth_body, others),
        [full] * 3,
        gx,
        gy,
        slope,
        fs,
        everyone,
        *slopes,
    )
    back_near = exchanged(g_near, "blk", near_pairs)
    grad_x, grad_y, row_loss = finish(
        others,
        3.0 * members * count,
        unit_x,
        scale_x,
        gx,
        *back_x,
        unit_y,
        scale_y,
        g_own,
        back_near,
        one,
        two,
        sums[0],
        *back_sum,
    )
    return (row_loss.reshape(count), grad_x, grad_y)


def solution(mesh):
    placed = (P(("blk", "grp"), None), P(("blk", "grp"), None), P(), P(), P(("blk", "grp")))
    return jax.shard_map(
        body,
        mesh=mesh,
        in_specs=placed,
        out_specs=(P(("blk", "grp")), P(("blk", "grp"), None), P(("blk", "grp"), None)),
        check_vma=False,
    )
```

```python
import functools

import jax
import jax.numpy as jnp
from jax import lax
from jax.experimental import pallas as pl
from jax.experimental.pallas import tpu as pltpu
from jax.sharding import PartitionSpec as P


BF = jnp.bfloat16
F32 = jnp.float32
VMEM = pl.BlockSpec(memory_space=pltpu.VMEM)
SMEM = pl.BlockSpec(memory_space=pltpu.SMEM)
HBM = pl.BlockSpec(memory_space=pltpu.HBM)
CHUNKS = 4
NT = ((1,), (1,))
NN = ((1,), (0,))


def exchanged(x, axis, pairs):
    return lax.ppermute(x, axis, pairs + [(b, a) for (a, b) in pairs])


def mixed_pairs(length, members):
    first, second = [], []
    for b in range(length):
        far = (b + 1) % length if b % 2 else (b - 1) % length
        for g in range(members):
            here = b * members + g
            across = (here, far * members + g)
            along = (here, b * members + (g + 1) % members)
            direct = length % 4 == 0 and b % 4 in (1, 2)
            first.append(across if direct else along)
            second.append(along if direct else across)
    return first, second


def far_goes_first():
    place = lax.axis_index("blk")
    return (lax.axis_size("blk") % 4 == 0) & (lax.rem(place + 1, 4) >= 2)


def shifted(x, axis, by):
    length = lax.axis_size(axis)
    return lax.ppermute(x, axis, [(i, (i + by) % length) for i in range(length)])


def stacked(v):
    high = v.astype(BF)
    return jnp.concatenate([high, (v - high.astype(F32)).astype(BF)], axis=0)


def mm(a, b, dims):
    rows = a.shape[0] // 2
    deep = b.shape[0] // 2

    def one(p, q):
        return lax.dot_general(p, q, (dims, ((), ())), preferred_element_type=F32)

    both = one(a[...], b[:deep])
    return both[:rows] + (both[rows:] + one(a[:rows], b[deep:]))


def log_one_plus(t):
    series = t * (1.0 + t * (-0.5 + t * (1.0 / 3.0 + t * (-0.25 + t * 0.2))))
    return jnp.where(t < 0.03125, series, jnp.log(1.0 + t))


def gated(z, weight, diagonal=None):
    signed = z if diagonal is None else jnp.where(diagonal, -z, z)
    small = jnp.exp(-jnp.abs(signed))
    loss = jnp.maximum(signed, 0.0) + log_one_plus(small)
    slope = jnp.where(signed >= 0.0, 1.0, small) / (1.0 + small) * weight
    if diagonal is not None:
        slope = jnp.where(diagonal, -slope, slope)
    return loss, slope


def scale_of(raw):
    return lax.rsqrt(jnp.sum(raw * raw, axis=1, keepdims=True) + 1e-06)


def square(count):
    rows = lax.broadcasted_iota(jnp.int32, (count, count), 0)
    return rows == lax.broadcasted_iota(jnp.int32, (count, count), 1)


def scalars_of(tb_ref):
    return tb_ref[0:1, 0:1], tb_ref[1:2, 0:1]


def first_body(lt, bi, x_any, y_any, near_ref, w_ref, *refs):
    tb_ref, x_ref, xc_ref, y_ref, yc_ref, xs_ref, ys_ref, gx_ref, gy_ref, sum_ref = refs[:10]
    sem = refs[10]
    copies = [
        pltpu.make_async_copy(x_any, x_ref, sem.at[0]),
        pltpu.make_async_copy(y_any, y_ref, sem.at[1]),
    ]
    for copy in copies:
        copy.start()
    count = near_ref.shape[0]
    near = near_ref[...] * scale_of(near_ref[...])
    for copy, ref, scale_ref in zip(copies, (x_ref, y_ref), (xc_ref, yc_ref)):
        copy.wait()
        scale_ref[...] = scale_of(ref[...])
        ref[...] = ref[...] * scale_ref[...]
    xs_ref[...] = stacked(x_ref[...])
    ys_ref[...] = stacked(jnp.concatenate([y_ref[...], near], axis=0))
    tb_ref[0:1, :] = jnp.exp(jnp.full((1, count), lt[0], F32))
    tb_ref[1:2, :] = jnp.full((1, count), bi[0], F32)
    temper, bias = scalars_of(tb_ref)
    rows = lax.broadcasted_iota(jnp.int32, (2 * count, count), 0)
    cols = lax.broadcasted_iota(jnp.int32, (2 * count, count), 1)
    z = temper * mm(ys_ref, xs_ref, NT) + bias
    loss, slope = gated(z, w_ref[...] * temper, rows == cols)
    sum_ref[...] = jnp.sum(loss, axis=0, keepdims=True)
    gx_ref[...] = mm(stacked(slope.T), ys_ref, NN)
    gy_ref[...] = mm(stacked(slope), xs_ref, NN)


def second_body(others, tb_ref, *refs):
    raw_refs, refs = refs[:others], refs[others:]
    w_refs, refs = refs[:others], refs[others:]
    xs_ref, ys_ref, all_ref, refs = *refs[:3], refs[3:]
    gp_refs, refs = refs[:others], refs[others:]
    sump_refs, slope_refs, row_refs = refs[:others], refs[others : 2 * others], refs[2 * others :]
    temper, bias = scalars_of(tb_ref)
    count = raw_refs[0].shape[0]
    deep = (others + 1) * count
    eye = square(count)
    all_ref[:count] = xs_ref[:count]
    all_ref[deep : deep + count] = xs_ref[count:]
    for s in range(others):
        raw = raw_refs[s][...]
        px = stacked(raw)
        scale = scale_of(raw)
        row_refs[s][...] = jnp.sum(jnp.where(eye, scale, 0.0), axis=0, keepdims=True)
        here = (s + 1) * count
        all_ref[here : here + count] = px[:count]
        all_ref[deep + here : deep + here + count] = px[count:]
        z = (temper * scale) * mm(px, ys_ref, NT) + bias
        weight = jnp.sum(jnp.where(eye, w_refs[s][...], 0.0), axis=1, keepdims=True)
        loss, slope = gated(z, weight * temper)
        sums = jnp.sum(loss, axis=1, keepdims=True)
        sump_refs[s][...] = jnp.sum(jnp.where(eye, sums, 0.0), axis=0, keepdims=True)
        slope_refs[s][...] = slope * scale
        gp_refs[s][...] = mm(stacked(slope), ys_ref, NN)


def third_body(others, tb_ref, *refs):
    members = others + 1
    far_ref, refs = refs[0], refs[1:]
    w_refs, refs = refs[:members], refs[members:]
    all_ref, gp_in, refs = *refs[:2], refs[2:]
    sum_in, refs = refs[:members], refs[members:]
    row_refs, refs = refs[:others], refs[others:]
    one_ref, refs = refs[0], refs[1:]
    sum_refs, refs = refs[:members], refs[members:]
    fs_ref, both_ref, slope_ref = refs
    temper, bias = scalars_of(tb_ref)
    count = far_ref.shape[0]
    far = far_ref[...]
    fs_ref[...] = stacked(far)
    scale = scale_of(far)
    along = jnp.concatenate([jnp.ones((1, count), F32), *[r[...] for r in row_refs]], axis=1)
    z = (temper * scale) * (along * mm(fs_ref, all_ref, NT)) + bias
    weight = jnp.concatenate([w[...] for w in w_refs], axis=1) * temper
    loss, slope = gated(z, weight)
    both_ref[...] = stacked(slope * along)
    slope = slope * scale
    sums = jnp.sum(loss, axis=0, keepdims=True)
    for s in range(members):
        part = slice(s * count, (s + 1) * count)
        sum_refs[s][...] = sum_in[s][...] + sums[:, part]
        slope_ref[s] = slope[:, part]

    @pl.when(far_goes_first())
    def _():
        one_ref[...] = mm(both_ref, all_ref, NN)

    @pl.when(jnp.logical_not(far_goes_first()))
    def _():
        one_ref[...] = gp_in[...] + mm(stacked(slope_ref[1].T), fs_ref, NN)


def rest_body(others, *refs):
    gp_in, (fs_ref, both_ref, slope_ref, all_ref, two_ref), gp_refs = (
        refs[:others],
        refs[others : others + 5],
        refs[others + 5 :],
    )

    @pl.when(far_goes_first())
    def _():
        two_ref[...] = gp_in[0][...] + mm(stacked(slope_ref[1].T), fs_ref, NN)

    @pl.when(jnp.logical_not(far_goes_first()))
    def _():
        two_ref[...] = mm(both_ref, all_ref, NN)

    for s in range(2, others + 1):
        gp_refs[s - 2][...] = gp_in[s - 1][...] + mm(stacked(slope_ref[s].T), fs_ref, NN)


def fourth_body(others, gx_in, gy_in, slope_ref, fs_ref, all_ref, *refs):
    slopes, (gx_ref, gown_ref, gnear_ref) = refs[:others], refs[others:]
    count = gx_in.shape[0]
    deep = (others + 1) * count
    gy = gy_in[...]
    for s in range(others):
        here = (s + 1) * count
        px = jnp.concatenate(
            [all_ref[here : here + count], all_ref[deep + here : deep + here + count]], axis=0
        )
        gy = gy + mm(stacked(slopes[s][...].T), px, NN)
    gown_ref[...] = gy[:count]
    gnear_ref[...] = gy[count:]
    gx_ref[...] = gx_in[...] + mm(stacked(slope_ref[0].T), fs_ref, NN)


def last_body(others, pairs, *refs):
    (unit_x, scale_x, own_x), refs = refs[:3], refs[3:]
    back_x, refs = refs[: others - 1], refs[others - 1 :]
    (unit_y, scale_y, own_y, near_y, one, two), refs = refs[:6], refs[6:]
    sums, refs = refs[: others + 1], refs[others + 1 :]
    x_out, y_out, loss_out, held, line, sem = refs
    rows = unit_x.shape[0] // CHUNKS
    total = sums[0][...]
    for r in sums[1:]:
        total = total + r[...]
    line[...] = total / pairs

    copies = [pltpu.make_async_copy(line, loss_out, sem.at[0])]
    copies[0].start()

    def side(k, unit_ref, scale_ref, grads, out_ref):
        for c in range(CHUNKS):
            here = pl.ds(c * rows, rows)
            grad = grads[0][here, :]
            for r in grads[1:]:
                grad = grad + r[here, :]
            unit = unit_ref[here, :]
            inner = jnp.sum(unit * grad, axis=1, keepdims=True)
            held[k, here, :] = scale_ref[here, :] * (grad - unit * inner)
            piece(k, c, out_ref).start()

    def piece(k, c, out_ref):
        here = pl.ds(c * rows, rows)
        return pltpu.make_async_copy(
            held.at[k, here, :], out_ref.at[here, :], sem.at[1 + k * CHUNKS + c]
        )

    far_first = far_goes_first()
    near_first = jnp.logical_not(far_first)
    sides = ((0, unit_x, scale_x, x_out), (1, unit_y, scale_y, y_out))
    mine = ([own_x, *back_x], [own_y, near_y])
    for (k, unit, scale, out), terms, early, late in zip(sides, mine, (two, one), (one, two)):
        pl.when(far_first)(functools.partial(side, k, unit, scale, [*terms, early], out))
        pl.when(near_first)(functools.partial(side, k, unit, scale, [*terms, late], out))
    copies += [piece(k, c, out) for k, _, _, out in sides for c in range(CHUNKS)]
    for copy in copies:
        copy.wait()


def shape(*dims, kind=F32):
    return jax.ShapeDtypeStruct(dims, kind)


PARAMS = pltpu.CompilerParams(vmem_limit_bytes=16 * 1024 * 1024)


def in_hbm(args):
    return [pltpu.with_memory_space_constraint(a, pltpu.HBM) for a in args]


def in_vmem(args):
    return [pltpu.with_memory_space_constraint(a, pltpu.VMEM) for a in args]


def call(body, outs, *args, scratch=(), scalars=0, anywhere=0):
    numbers, args = args[:scalars], args[scalars:]
    return pl.pallas_call(
        body,
        out_shape=[pltpu.VMEM(o.shape, o.dtype) for o in outs],
        in_specs=[SMEM] * scalars + [HBM] * anywhere + [VMEM] * (len(args) - anywhere),
        out_specs=[VMEM] * len(outs),
        scratch_shapes=list(scratch),
        compiler_params=PARAMS,
    )(*numbers, *in_hbm(args[:anywhere]), *in_vmem(args[anywhere:]))


def finish(others, pairs, *args):
    full = shape(*args[0].shape)
    line = shape(1, full.shape[0])
    return pl.pallas_call(
        functools.partial(last_body, others, pairs),
        out_shape=[full, full, line],
        in_specs=[VMEM] * len(args),
        out_specs=[HBM] * 3,
        scratch_shapes=[
            pltpu.VMEM((2, *full.shape), F32),
            pltpu.VMEM(line.shape, F32),
            pltpu.SemaphoreType.DMA((2 * CHUNKS + 1,)),
        ],
        compiler_params=PARAMS,
    )(*in_vmem(args))


def body(images, texts, log_temp, bias, row_weight):
    members = lax.axis_size("grp")
    others = members - 1
    count, width = images.shape
    weight = row_weight.reshape(1, count)
    length = lax.axis_size("blk")
    near_pairs = [(i, i + 1) for i in range(0, length, 2)]
    far_pairs = [(i, (i + 1) % length) for i in range(1, length, 2)]
    raws = [shifted(images, "grp", -s) for s in range(1, members)]
    far = exchanged(texts, "blk", far_pairs)
    near = exchanged(texts, "blk", near_pairs)
    weights = [weight] + [shifted(weight, "grp", -s) for s in range(1, members)]
    full = shape(count, width)
    line = shape(1, count)
    stack = shape(2 * count, width, kind=BF)
    tb, unit_x, scale_x, unit_y, scale_y, xs, ys, gx, gy, sums = call(
        first_body,
        [
            shape(2, count),
            full,
            shape(count, 1),
            full,
            shape(count, 1),
            stack,
            shape(4 * count, width, kind=BF),
            full,
            shape(2 * count, width),
            line,
        ],
        log_temp,
        bias,
        images,
        texts,
        near,
        weight,
        scratch=[pltpu.SemaphoreType.DMA((2,))],
        scalars=2,
        anywhere=2,
    )
    outs = call(
        functools.partial(second_body, others),
        [shape(2 * members * count, width, kind=BF)]
        + [full] * others
        + [line] * others
        + [shape(count, 2 * count)] * others
        + [line] * others,
        tb,
        *raws,
        *weights[1:],
        xs,
        ys,
    )
    everyone, outs = outs[0], outs[1:]
    gp, outs = outs[:others], outs[others:]
    sump, slopes, rows = outs[:others], outs[others : 2 * others], outs[2 * others :]
    outs = call(
        functools.partial(third_body, others),
        [full]
        + [line] * members
        + [
            stack,
            shape(2 * count, members * count, kind=BF),
            shape(members, count, count),
        ],
        tb,
        far,
        *weights,
        everyone,
        gp[0],
        sums,
        *sump,
        *rows,
    )
    one, outs = outs[0], outs[1:]
    sums, (fs, both, slope) = outs[:members], outs[members:]
    first, second = mixed_pairs(length, members)
    one = lax.ppermute(one, ("blk", "grp"), first)
    two, *gp = call(
        functools.partial(rest_body, others),
        [full] * others,
        *gp,
        fs,
        both,
        slope,
        everyone,
    )
    two = lax.ppermute(two, ("blk", "grp"), second)
    back_x = [shifted(gp[s - 2], "grp", s) for s in range(2, members)]
    back_sum = [shifted(sums[s], "grp", s) for s in range(1, members)]
    gx, g_own, g_near = call(
        functools.partial(fourth_body, others),
        [full] * 3,
        gx,
        gy,
        slope,
        fs,
        everyone,
        *slopes,
    )
    back_near = exchanged(g_near, "blk", near_pairs)
    grad_x, grad_y, row_loss = finish(
        others,
        3.0 * members * count,
        unit_x,
        scale_x,
        gx,
        *back_x,
        unit_y,
        scale_y,
        g_own,
        back_near,
        one,
        two,
        sums[0],
        *back_sum,
    )
    return (row_loss.reshape(count), grad_x, grad_y)


def solution(mesh):
    placed = (P(("blk", "grp"), None), P(("blk", "grp"), None), P(), P(), P(("blk", "grp")))
    return jax.shard_map(
        body,
        mesh=mesh,
        in_specs=placed,
        out_specs=(P(("blk", "grp")), P(("blk", "grp"), None), P(("blk", "grp"), None)),
        check_vma=False,
    )
```

```python
import functools

import jax
import jax.numpy as jnp
from jax import lax
from jax.experimental import pallas as pl
from jax.experimental.pallas import tpu as pltpu
from jax.sharding import PartitionSpec as P


BF = jnp.bfloat16
F32 = jnp.float32
VMEM = pl.BlockSpec(memory_space=pltpu.VMEM)
SMEM = pl.BlockSpec(memory_space=pltpu.SMEM)
HBM = pl.BlockSpec(memory_space=pltpu.HBM)
CHUNKS = 4
NT = ((1,), (1,))
NN = ((1,), (0,))


def exchanged(x, axis, pairs):
    return lax.ppermute(x, axis, pairs + [(b, a) for (a, b) in pairs])


def mixed_pairs(length, members):
    first, second = [], []
    for b in range(length):
        far = (b + 1) % length if b % 2 else (b - 1) % length
        for g in range(members):
            here = b * members + g
            across = (here, far * members + g)
            along = (here, b * members + (g + 1) % members)
            direct = length % 4 == 0 and b % 4 in (1, 2)
            first.append(across if direct else along)
            second.append(along if direct else across)
    return first, second


def far_goes_first():
    place = lax.axis_index("blk")
    return (lax.axis_size("blk") % 4 == 0) & (lax.rem(place + 1, 4) >= 2)


def shifted(x, axis, by):
    length = lax.axis_size(axis)
    return lax.ppermute(x, axis, [(i, (i + by) % length) for i in range(length)])


def stacked(v):
    high = v.astype(BF)
    return jnp.concatenate([high, (v - high.astype(F32)).astype(BF)], axis=0)


def mm(a, b, dims):
    rows = a.shape[0] // 2
    deep = b.shape[0] // 2

    def one(p, q):
        return lax.dot_general(p, q, (dims, ((), ())), preferred_element_type=F32)

    both = one(a[...], b[:deep])
    return both[:rows] + (both[rows:] + one(a[:rows], b[deep:]))


def log_one_plus(t):
    series = t * (1.0 + t * (-0.5 + t * (1.0 / 3.0 + t * (-0.25 + t * 0.2))))
    return jnp.where(t < 0.03125, series, jnp.log(1.0 + t))


def gated(z, weight, diagonal=None):
    signed = z if diagonal is None else jnp.where(diagonal, -z, z)
    small = jnp.exp(-jnp.abs(signed))
    loss = jnp.maximum(signed, 0.0) + log_one_plus(small)
    slope = jnp.where(signed >= 0.0, 1.0, small) / (1.0 + small) * weight
    if diagonal is not None:
        slope = jnp.where(diagonal, -slope, slope)
    return loss, slope


def scale_of(raw):
    return lax.rsqrt(jnp.sum(raw * raw, axis=1, keepdims=True) + 1e-06)


def square(count):
    rows = lax.broadcasted_iota(jnp.int32, (count, count), 0)
    return rows == lax.broadcasted_iota(jnp.int32, (count, count), 1)


def scalars_of(tb_ref):
    return tb_ref[0:1, 0:1], tb_ref[1:2, 0:1]


def first_body(lt, bi, x_any, y_any, near_ref, w_ref, *refs):
    tb_ref, x_ref, xc_ref, y_ref, yc_ref, xs_ref, ys_ref, gx_ref, gy_ref, sum_ref = refs[:10]
    sem = refs[10]
    copies = [
        pltpu.make_async_copy(x_any, x_ref, sem.at[0]),
        pltpu.make_async_copy(y_any, y_ref, sem.at[1]),
    ]
    for copy in copies:
        copy.start()
    count = near_ref.shape[0]
    near = near_ref[...] * scale_of(near_ref[...])
    for copy, ref, scale_ref in zip(copies, (x_ref, y_ref), (xc_ref, yc_ref)):
        copy.wait()
        scale_ref[...] = scale_of(ref[...])
        ref[...] = ref[...] * scale_ref[...]
    xs_ref[...] = stacked(x_ref[...])
    ys_ref[...] = stacked(jnp.concatenate([y_ref[...], near], axis=0))
    tb_ref[0:1, :] = jnp.exp(jnp.full((1, count), lt[0], F32))
    tb_ref[1:2, :] = jnp.full((1, count), bi[0], F32)
    temper, bias = scalars_of(tb_ref)
    rows = lax.broadcasted_iota(jnp.int32, (2 * count, count), 0)
    cols = lax.broadcasted_iota(jnp.int32, (2 * count, count), 1)
    z = temper * mm(ys_ref, xs_ref, NT) + bias
    loss, slope = gated(z, w_ref[...] * temper, rows == cols)
    sum_ref[...] = jnp.sum(loss, axis=0, keepdims=True)
    gx_ref[...] = mm(stacked(slope.T), ys_ref, NN)
    gy_ref[...] = mm(stacked(slope), xs_ref, NN)


def second_body(others, tb_ref, *refs):
    raw_refs, refs = refs[:others], refs[others:]
    w_refs, refs = refs[:others], refs[others:]
    xs_ref, ys_ref, all_ref, refs = *refs[:3], refs[3:]
    gp_refs, refs = refs[:others], refs[others:]
    sump_refs, slope_refs, row_refs = refs[:others], refs[others : 2 * others], refs[2 * others :]
    temper, bias = scalars_of(tb_ref)
    count = raw_refs[0].shape[0]
    deep = (others + 1) * count
    eye = square(count)
    all_ref[:count] = xs_ref[:count]
    all_ref[deep : deep + count] = xs_ref[count:]
    for s in range(others):
        raw = raw_refs[s][...]
        px = stacked(raw)
        scale = scale_of(raw)
        row_refs[s][...] = jnp.sum(jnp.where(eye, scale, 0.0), axis=0, keepdims=True)
        here = (s + 1) * count
        all_ref[here : here + count] = px[:count]
        all_ref[deep + here : deep + here + count] = px[count:]
        z = (temper * scale) * mm(px, ys_ref, NT) + bias
        weight = jnp.sum(jnp.where(eye, w_refs[s][...], 0.0), axis=1, keepdims=True)
        loss, slope = gated(z, weight * temper)
        sums = jnp.sum(loss, axis=1, keepdims=True)
        sump_refs[s][...] = jnp.sum(jnp.where(eye, sums, 0.0), axis=0, keepdims=True)
        slope_refs[s][...] = slope * scale
        gp_refs[s][...] = mm(stacked(slope), ys_ref, NN)


def third_body(others, tb_ref, *refs):
    members = others + 1
    far_ref, refs = refs[0], refs[1:]
    w_refs, refs = refs[:members], refs[members:]
    all_ref, refs = refs[0], refs[1:]
    gp_in, refs = refs[:others], refs[others:]
    sum_in, refs = refs[:members], refs[members:]
    row_refs, refs = refs[:others], refs[others:]
    one_ref, two_ref, refs = *refs[:2], refs[2:]
    gp_refs, refs = refs[: others - 1], refs[others - 1 :]
    sum_refs, refs = refs[:members], refs[members:]
    fs_ref, slope_ref, both_ref, turned_ref = refs
    temper, bias = scalars_of(tb_ref)
    count = far_ref.shape[0]
    far = far_ref[...]
    fs_ref[...] = stacked(far)
    scale = scale_of(far)
    along = jnp.concatenate([jnp.ones((1, count), F32), *[r[...] for r in row_refs]], axis=1)
    z = (temper * scale) * (along * mm(fs_ref, all_ref, NT)) + bias
    weight = jnp.concatenate([w[...] for w in w_refs], axis=1) * temper
    loss, slope = gated(z, weight)
    both_ref[...] = stacked(slope * along)
    slope = slope * scale
    sums = jnp.sum(loss, axis=0, keepdims=True)
    for s in range(members):
        part = slice(s * count, (s + 1) * count)
        sum_refs[s][...] = sum_in[s][...] + sums[:, part]
        if s == 0:
            slope_ref[...] = slope[:, part]
        else:
            turned_ref[s - 1] = stacked(slope[:, part].T)
            if s > 1:
                gp_refs[s - 2][...] = gp_in[s - 1][...] + mm(turned_ref[s - 1], fs_ref, NN)

    def finish_into(far_out, next_out):
        far_out[...] = mm(both_ref, all_ref, NN)
        next_out[...] = gp_in[0][...] + mm(turned_ref[0], fs_ref, NN)

    far_first = far_goes_first()
    pl.when(far_first)(lambda: finish_into(one_ref, two_ref))
    pl.when(jnp.logical_not(far_first))(lambda: finish_into(two_ref, one_ref))


def fourth_body(others, gx_in, gy_in, slope_ref, fs_ref, all_ref, *refs):
    slopes, (gx_ref, gown_ref, gnear_ref) = refs[:others], refs[others:]
    count = gx_in.shape[0]
    deep = (others + 1) * count
    gy = gy_in[...]
    for s in range(others):
        here = (s + 1) * count
        px = jnp.concatenate(
            [all_ref[here : here + count], all_ref[deep + here : deep + here + count]], axis=0
        )
        gy = gy + mm(stacked(slopes[s][...].T), px, NN)
    gown_ref[...] = gy[:count]
    gnear_ref[...] = gy[count:]
    gx_ref[...] = gx_in[...] + mm(stacked(slope_ref[...].T), fs_ref, NN)


def last_body(others, pairs, *refs):
    (unit_x, scale_x, own_x), refs = refs[:3], refs[3:]
    back_x, refs = refs[: others - 1], refs[others - 1 :]
    (unit_y, scale_y, own_y, near_y, one, two), refs = refs[:6], refs[6:]
    sums, refs = refs[: others + 1], refs[others + 1 :]
    x_out, y_out, loss_out, held, line, sem = refs
    rows = unit_x.shape[0] // CHUNKS
    total = sums[0][...]
    for r in sums[1:]:
        total = total + r[...]
    line[...] = total / pairs

    def run(far_y, next_x):
        copies = []

        def send(source, target):
            copies.append(pltpu.make_async_copy(source, target, sem.at[len(copies)]))
            copies[-1].start()

        send(line, loss_out)
        sides = [
            (unit_x, scale_x, [own_x, next_x, *back_x], x_out),
            (unit_y, scale_y, [own_y, near_y, far_y], y_out),
        ]
        for k, (unit_ref, scale_ref, grads, out_ref) in enumerate(sides):
            for c in range(CHUNKS):
                here = pl.ds(c * rows, rows)
                grad = grads[0][here, :]
                for r in grads[1:]:
                    grad = grad + r[here, :]
                unit = unit_ref[here, :]
                inner = jnp.sum(unit * grad, axis=1, keepdims=True)
                held[k, here, :] = scale_ref[here, :] * (grad - unit * inner)
                send(held.at[k, here, :], out_ref.at[here, :])
        for copy in copies:
            copy.wait()

    far_first = far_goes_first()
    pl.when(far_first)(lambda: run(one, two))
    pl.when(jnp.logical_not(far_first))(lambda: run(two, one))


def shape(*dims, kind=F32):
    return jax.ShapeDtypeStruct(dims, kind)


PARAMS = pltpu.CompilerParams(vmem_limit_bytes=16 * 1024 * 1024)


def in_hbm(args):
    return [pltpu.with_memory_space_constraint(a, pltpu.HBM) for a in args]


def in_vmem(args):
    return [pltpu.with_memory_space_constraint(a, pltpu.VMEM) for a in args]


def call(body, outs, *args, scratch=(), scalars=0, anywhere=0):
    numbers, args = args[:scalars], args[scalars:]
    return pl.pallas_call(
        body,
        out_shape=[pltpu.VMEM(o.shape, o.dtype) for o in outs],
        in_specs=[SMEM] * scalars + [HBM] * anywhere + [VMEM] * (len(args) - anywhere),
        out_specs=[VMEM] * len(outs),
        scratch_shapes=list(scratch),
        compiler_params=PARAMS,
    )(*numbers, *in_hbm(args[:anywhere]), *in_vmem(args[anywhere:]))


def finish(others, pairs, *args):
    full = shape(*args[0].shape)
    line = shape(1, full.shape[0])
    return pl.pallas_call(
        functools.partial(last_body, others, pairs),
        out_shape=[full, full, line],
        in_specs=[VMEM] * len(args),
        out_specs=[HBM] * 3,
        scratch_shapes=[
            pltpu.VMEM((2, *full.shape), F32),
            pltpu.VMEM(line.shape, F32),
            pltpu.SemaphoreType.DMA((2 * CHUNKS + 1,)),
        ],
        compiler_params=PARAMS,
    )(*in_vmem(args))


def body(images, texts, log_temp, bias, row_weight):
    members = lax.axis_size("grp")
    others = members - 1
    count, width = images.shape
    weight = row_weight.reshape(1, count)
    length = lax.axis_size("blk")
    near_pairs = [(i, i + 1) for i in range(0, length, 2)]
    far_pairs = [(i, (i + 1) % length) for i in range(1, length, 2)]
    raws = [shifted(images, "grp", -s) for s in range(1, members)]
    far = exchanged(texts, "blk", far_pairs)
    near = exchanged(texts, "blk", near_pairs)
    weights = [weight] + [shifted(weight, "grp", -s) for s in range(1, members)]
    full = shape(count, width)
    line = shape(1, count)
    stack = shape(2 * count, width, kind=BF)
    tb, unit_x, scale_x, unit_y, scale_y, xs, ys, gx, gy, sums = call(
        first_body,
        [
            shape(2, count),
            full,
            shape(count, 1),
            full,
            shape(count, 1),
            stack,
            shape(4 * count, width, kind=BF),
            full,
            shape(2 * count, width),
            line,
        ],
        log_temp,
        bias,
        images,
        texts,
        near,
        weight,
        scratch=[pltpu.SemaphoreType.DMA((2,))],
        scalars=2,
        anywhere=2,
    )
    outs = call(
        functools.partial(second_body, others),
        [shape(2 * members * count, width, kind=BF)]
        + [full] * others
        + [line] * others
        + [shape(count, 2 * count)] * others
        + [line] * others,
        tb,
        *raws,
        *weights[1:],
        xs,
        ys,
    )
    everyone, outs = outs[0], outs[1:]
    gp, outs = outs[:others], outs[others:]
    sump, slopes, rows = outs[:others], outs[others : 2 * others], outs[2 * others :]
    outs = call(
        functools.partial(third_body, others),
        [full, full]
        + [full] * (others - 1)
        + [line] * members
        + [stack, shape(count, count)],
        tb,
        far,
        *weights,
        everyone,
        *gp,
        sums,
        *sump,
        *rows,
        scratch=[
            pltpu.VMEM((2 * count, members * count), BF),
            pltpu.VMEM((others, 2 * count, count), BF),
        ],
    )
    one, two, outs = outs[0], outs[1], outs[2:]
    gp, outs = outs[: others - 1], outs[others - 1 :]
    sums, (fs, slope) = outs[:members], outs[members:]
    first, second = mixed_pairs(length, members)
    one = lax.ppermute(one, ("blk", "grp"), first)
    two = lax.ppermute(two, ("blk", "grp"), second)
    back_x = [shifted(gp[s - 2], "grp", s) for s in range(2, members)]
    back_sum = [shifted(sums[s], "grp", s) for s in range(1, members)]
    gx, g_own, g_near = call(
        functools.partial(fourth_body, others),
        [full] * 3,
        gx,
        gy,
        slope,
        fs,
        everyone,
        *slopes,
    )
    back_near = exchanged(g_near, "blk", near_pairs)
    grad_x, grad_y, row_loss = finish(
        others,
        3.0 * members * count,
        unit_x,
        scale_x,
        gx,
        *back_x,
        unit_y,
        scale_y,
        g_own,
        back_near,
        one,
        two,
        sums[0],
        *back_sum,
    )
    return (row_loss.reshape(count), grad_x, grad_y)


def solution(mesh):
    placed = (P(("blk", "grp"), None), P(("blk", "grp"), None), P(), P(), P(("blk", "grp")))
    return jax.shard_map(
        body,
        mesh=mesh,
        in_specs=placed,
        out_specs=(P(("blk", "grp")), P(("blk", "grp"), None), P(("blk", "grp"), None)),
        check_vma=False,
    )
```
